512 devices in a mesh: ctx: 64 (over x, z, core), head: 8 (over y).
Axes of the slice: x: 4, y: 8, z: 8, core: 2. Of those that a mesh axis runs over, the one named last changes fastest.
Arguments:
- queries: bfloat16 [12288, 4096], P('ctx', 'head'), may hold values from -6 to 6
- key_rows: bfloat16 [12288, 4096], P('ctx', 'head'), may hold values from -6 to 6
- value_rows: bfloat16 [12288, 4096], P('ctx', 'head'), may hold values from -120 to 120
- gate_rows: bfloat16 [12288, 4096], P('ctx', 'head'), may hold values from -8 to 8
- cotangent: bfloat16 [12288, 4096], P('ctx', 'head'), may hold values from -6 to 6
Outputs:
- grad_queries: bfloat16 [12288, 4096], P('ctx', 'head')
- grad_keys: bfloat16 [12288, 4096], P('ctx', 'head')
- grad_values: bfloat16 [12288, 4096], P('ctx', 'head')
- grad_gates: bfloat16 [12288, 4096], P('ctx', 'head')
The draws below stay inside these ranges and needn't reach their ends.
All inputs are finite; a program needn't handle non-finite values.
Results may differ from the reference program's by a relative error of at most 0.0065.
Values sent between devices are 32-bit elements; how exact they have to be, the bound alone decides.
A program may use at most 64 MiB of HBM per device.

```python
import jax
import jax.numpy as jnp
from jax import lax

H = 32
DH = 128
TOK_DEV = 192
HD = 4096
TOKENS = 12288
N_CTX = 64


def draw_value_rows(key, part):
    first, second, third = jax.random.split(key, 3)
    width = H * DH
    row_scale = jnp.exp(jax.random.uniform(second, (TOKENS, 1), jnp.float32) * jnp.log(10.0))
    base = jnp.clip(jax.random.normal(first, (TOKENS, width), jnp.float32), -4.0, 4.0)
    jitter = jnp.exp(jax.random.uniform(third, (1, width), jnp.float32) * jnp.log(3.0))
    head_index = (jnp.arange(width) // DH).astype(jnp.float32)[None, :]
    ramp = jnp.exp(jnp.log(4.0) * head_index / (H - 1))
    col_scale = jitter * ramp
    return (base * row_scale * col_scale / 4.0).astype(jnp.bfloat16)


def block_scale(stream_key, shape, cuts, smallest, top_value):
    def one(axis_at, blocks):
        steps = jax.random.uniform(jax.random.fold_in(jax.random.fold_in(stream_key, 6), axis_at), (blocks,), jnp.float32, smallest / len(cuts), top_value / len(cuts))
        return jnp.repeat(jnp.exp(steps), shape[axis_at] // blocks).reshape((-1,) + (1,) * (len(shape) - axis_at - 1))

    loudness = one(*cuts[0])
    for cut in cuts[1:]:
        loudness = loudness * one(*cut)
    return loudness


def centred(stream_key, extent, scale, most, cuts=(), kind=jnp.bfloat16):
    factor_of = block_scale(stream_key, extent, cuts, -0.22, 0.18) if cuts else 1.0
    values = jax.random.normal(stream_key, extent, jnp.float32) * scale * factor_of
    return jnp.minimum(jnp.maximum(values, -most), most).astype(kind)


def setup_inputs(seed: int = 0) -> dict:
    key_list = jax.random.split(jax.random.key(seed), 6)
    queries = centred(key_list[0], (TOKENS, HD), 1.0, 6.0, ((0, 64), (1, 8)))
    key_rows = centred(key_list[1], (TOKENS, HD), 1.0, 6.0, ((0, 64), (1, 8)))
    value_rows = draw_value_rows(jax.random.fold_in(key_list[5], 71), 0)
    gate_rows = centred(key_list[3], (TOKENS, HD), 2.0, 8.0, ((0, 64), (1, 8)))
    cotangent = centred(key_list[4], (TOKENS, HD), 1.0, 6.0, ((0, 64), (1, 8)))
    return {"queries": queries, "key_rows": key_rows, "value_rows": value_rows, "gate_rows": gate_rows, "cotangent": cotangent}


EPSILON = 1e-06
HIGH = lax.Precision.HIGHEST

def silu_slope(x):
    sig = jax.nn.sigmoid(x)
    return sig * (1.0 + x * (1.0 - sig))

def low_round(x):
    return lax.optimization_barrier(x.astype(jnp.bfloat16)).astype(jnp.float32)

def reference(queries, key_rows, value_rows, gate_rows, cotangent):
    width = H * DH
    q_float = queries.astype(jnp.float32)
    k_float = key_rows.astype(jnp.float32)
    lifted_q = jax.nn.silu(q_float).astype(jnp.bfloat16)
    lifted_k = jax.nn.silu(k_float).astype(jnp.bfloat16)

    def split(x):
        return x.astype(jnp.float32).reshape(N_CTX, TOK_DEV, H, DH)
    blocks_q = split(lifted_q)
    blocks_k = split(lifted_k)
    blocks_v = split(value_rows)
    causal = (lax.broadcasted_iota(jnp.int32, (TOK_DEV, TOK_DEV), 0) >= lax.broadcasted_iota(jnp.int32, (TOK_DEV, TOK_DEV), 1)).astype(jnp.float32)

    def forward(state, block):
        bq, bk, bv = block
        scores = jnp.einsum('thd,shd->hts', bq, bk, precision=HIGH) * causal[None]
        weights = low_round(scores)
        state_low = low_round(state)
        out = jnp.einsum('hts,shd->thd', weights, bv, precision=HIGH) + jnp.einsum('thd,hde->the', bq, state_low, precision=HIGH)
        local = jnp.einsum('thd,the->hde', bk, bv, precision=HIGH)
        return (state + local, (out, state))
    zero_state = jnp.zeros((H, DH, DH), jnp.float32)
    final, (outs, states) = lax.scan(forward, zero_state, (blocks_q, blocks_k, blocks_v))
    attended = outs.reshape(TOKENS, width)
    sumsq = lax.optimization_barrier(jnp.sum(attended * attended, axis=1, keepdims=True))
    rms = jnp.sqrt(sumsq / width + EPSILON)
    normed = attended / rms
    sig = jax.nn.sigmoid(gate_rows.astype(jnp.float32))
    grad_out = cotangent.astype(jnp.float32)
    grad_gates = (grad_out * normed * sig * (1.0 - sig)).astype(jnp.bfloat16)
    gated = grad_out * sig
    inner = lax.optimization_barrier(jnp.sum(gated * normed, axis=1, keepdims=True))
    d_attn = ((gated - normed * inner / width) / rms).astype(jnp.bfloat16)
    blocks_d = split(d_attn)

    def backward(carry, block):
        bq, bk, bv, bd, state = block
        scores = jnp.einsum('thd,shd->hts', bq, bk, precision=HIGH) * causal[None]
        weights = low_round(scores)
        d_scores = jnp.einsum('the,she->hts', bd, bv, precision=HIGH) * causal[None]
        d_weights = low_round(d_scores)
        state_low = low_round(state)
        carry_low = low_round(carry)
        grad_lq = jnp.einsum('hts,shd->thd', d_weights, bk, precision=HIGH) + jnp.einsum('the,hde->thd', bd, state_low, precision=HIGH)
        grad_lk = jnp.einsum('hts,thd->shd', d_weights, bq, precision=HIGH) + jnp.einsum('she,hde->shd', bv, carry_low, precision=HIGH)
        grad_v = jnp.einsum('hts,the->she', weights, bd, precision=HIGH) + jnp.einsum('shd,hde->she', bk, carry_low, precision=HIGH)
        local = jnp.einsum('thd,the->hde', bq, bd, precision=HIGH)
        return (carry + local, (grad_lq, grad_lk, grad_v))
    last, (gq, gk, gv) = lax.scan(backward, zero_state, (blocks_q, blocks_k, blocks_v, blocks_d, states), reverse=True)
    grad_queries = (gq.reshape(TOKENS, width) * silu_slope(q_float)).astype(jnp.bfloat16)
    grad_keys = (gk.reshape(TOKENS, width) * silu_slope(k_float)).astype(jnp.bfloat16)
    grad_values = gv.reshape(TOKENS, width).astype(jnp.bfloat16)
    return (grad_queries, grad_keys, grad_values, grad_gates)
```

```python
import functools

import jax
import jax.numpy as jnp
from jax import lax
from jax.experimental import pallas as pl
from jax.experimental.pallas import tpu as pltpu
from jax.sharding import PartitionSpec as P

H = 32
DH = 128
EPSILON = 1e-06
NZ = 8
F32 = jnp.float32
BF16 = jnp.bfloat16

NN = (((1,), (0,)), ((), ()))
NT = (((1,), (1,)), ((), ()))
TN = (((0,), (0,)), ((), ()))


def mm(a, b, dims):
    return lax.dot_general(a, b, dims, preferred_element_type=F32)


def silu_slope(x):
    sig = jax.nn.sigmoid(x)
    return sig * (1.0 + x * (1.0 - sig))


def kernel(
    nx, nz, nh,
    q_hbm, k_hbm, v_hbm, g_hbm, c_hbm,
    oq, ok, ov, og,
    q_ref, k_ref, v_ref, g_ref, c_ref,
    lq_ref, lk_ref, da_ref, wt_ref,
    att, gated, gg, glk, gv,
    st1, st2,
    loc, x_in, comb, a_in, p_out, e_in, f_out, f_in,
    y_out, y_in,
    in_sem, out_sem, send_sem, recv_sem, ysem,
    oq_ref, ok_ref, ov_ref, og_ref,
):
    rows, width = q_ref.shape
    heads = width // DH
    chips = nx * nz
    half = heads * DH // 2
    piece = half // chips
    me = lax.axis_index("ctx")
    hd = lax.axis_index("head")
    core = lax.rem(me, 2)
    chip = lax.div(me, 2)
    cx = lax.div(chip, nz)
    cz = lax.rem(chip, nz)
    partner = chip * 2 + (1 - core)

    ins = [
        pltpu.make_async_copy(src, dst, in_sem.at[i])
        for i, (src, dst) in enumerate(
            ((k_hbm, k_ref), (v_hbm, v_ref), (q_hbm, q_ref), (g_hbm, g_ref), (c_hbm, c_ref))
        )
    ]
    for copy in ins:
        copy.start()

    def far(i, n):
        odd = lax.rem(i, 2)
        return n // 2 + lax.div(i + 1, 2) * (1 - 2 * odd)

    def other_chip(step):
        dz = far(lax.div(step, nx), nz)
        dx = far(lax.rem(step, nx), nx)
        return lax.rem(cx + dx, nx) * nz + lax.rem(cz + dz, nz)

    barrier = pltpu.get_barrier_semaphore()

    def greet(step, carry):
        pl.semaphore_signal(barrier, inc=1, device_id={"ctx": other_chip(step) * 2 + core})
        return carry

    lax.fori_loop(0, chips - 1, greet, 0)

    def greet_head(step, carry):
        pl.semaphore_signal(barrier, inc=1, device_id={"head": lax.rem(hd + step, nh)})
        return carry

    lax.fori_loop(1, nh, greet_head, 0)
    pl.semaphore_signal(barrier, inc=1, device_id={"ctx": partner})

    def hs(h):
        return slice(h * DH, (h + 1) * DH)

    def remote(src, dst, scan, stage, device):
        return pltpu.make_async_remote_copy(
            src_ref=src,
            dst_ref=dst,
            send_sem=send_sem.at[scan, stage],
            recv_sem=recv_sem.at[scan, stage],
            device_id=device,
        )

    def scatter(src, dst, scan, stage):
        def one(step, carry):
            to = other_chip(step)
            remote(src.at[to], dst.at[chip], scan, stage, {"ctx": to * 2 + core}).start()
            return carry

        lax.fori_loop(0, chips - 1, one, 0)

    def scattered(src, dst, scan, stage):
        n = pl.ds(0, chips - 1)
        return remote(src.at[n], dst.at[n], scan, stage, {"ctx": partner})

    my_half = pl.ds(pl.multiple_of(core * half, half), half)
    other_half = pl.ds(pl.multiple_of((1 - core) * half, half), half)

    def scan_pair(scan):
        copy = remote(loc.at[scan, other_half], x_in.at[scan], scan, 0, {"ctx": partner})
        copy.start()
        return copy

    def scan_out(scan, pair):
        pair.wait_recv()
        both = loc[scan, my_half] + x_in[scan]
        comb[scan] = both.reshape(chips, piece, DH)
        scatter(comb.at[scan], a_in.at[scan], scan, 1)
        a_in[scan, chip] = comb[scan, chip]
        return scattered(comb.at[scan], a_in.at[scan], scan, 1)

    def scan_back(scan, first, reverse):
        first.wait_recv()
        total = jnp.zeros((piece, DH), F32)
        for i in range(chips):
            j = chips - 1 - i if reverse else i
            p_out[scan, j] = total
            total = total + a_in[scan, j]
        scatter(p_out.at[scan], e_in.at[scan], scan, 2)
        e_in[scan, chip] = p_out[scan, chip]
        return scattered(p_out.at[scan], e_in.at[scan], scan, 2)

    def scan_end(scan, second, reverse, state):
        second.wait_recv()
        later = 0 if reverse else 1
        mine = e_in[scan].reshape(half, DH)
        f_out[scan] = mine + jnp.where(core == later, 0.0, loc[scan, my_half])
        last = remote(f_out.at[scan], f_in.at[scan], scan, 3, {"ctx": partner})
        last.start()
        state[my_half] = (mine + jnp.where(core == later, x_in[scan], 0.0)).astype(BF16)
        last.wait_recv()
        state[other_half] = f_in[scan].astype(BF16)
        return last

    ins[0].wait()
    kf = k_ref[...].astype(F32)
    lk_ref[...] = jax.nn.silu(kf).astype(BF16)
    ins[1].wait()
    for h in range(heads):
        loc[0, hs(h)] = mm(lk_ref[:, hs(h)], v_ref[:, hs(h)], TN)
    pl.semaphore_wait(barrier, chips - 1 + 1 + nh - 1)
    pair1 = scan_pair(0)
    y_out[...] = jnp.zeros_like(y_out)
    first1 = scan_out(0, pair1)

    row = lax.broadcasted_iota(jnp.int32, (rows, rows), 0)
    col = lax.broadcasted_iota(jnp.int32, (rows, rows), 1)
    ins[2].wait()
    qf = q_ref[...].astype(F32)
    lq_ref[...] = jax.nn.silu(qf).astype(BF16)
    for h in range(heads):
        lq, lk, v = lq_ref[:, hs(h)], lk_ref[:, hs(h)], v_ref[:, hs(h)]
        w = jnp.where(row >= col, mm(lq, lk, NT), 0.0).astype(BF16)
        att[:, hs(h)] = mm(w, v, NN)
    second1 = scan_back(0, first1, False)
    ins[3].wait()
    ins[4].wait()
    sig = jax.nn.sigmoid(g_ref[...].astype(F32))
    gat = c_ref[...].astype(F32) * sig
    gated[...] = gat
    gg[...] = gat * (1.0 - sig)
    for h in range(heads):
        lq, lk = lq_ref[:, hs(h)], lk_ref[:, hs(h)]
        wt_ref[h] = jnp.where(col >= row, mm(lk, lq, NT), 0.0).astype(BF16)
    last1 = scan_end(0, second1, False, st1)

    sq = jnp.zeros((rows, DH), F32)
    dt = jnp.zeros((rows, DH), F32)
    for h in range(heads):
        a = att[:, hs(h)] + mm(lq_ref[:, hs(h)], st1[hs(h)], NN)
        att[:, hs(h)] = a
        sq = sq + a * a
        dt = dt + gated[:, hs(h)] * a

    def to_lanes(part):
        column = jnp.sum(part, axis=1, keepdims=True)
        return jnp.sum(jnp.where(row == col, column, 0.0), axis=0, keepdims=True)

    y_out[:, 0:rows] = to_lanes(sq)
    y_out[:, 256 : 256 + rows] = to_lanes(dt)

    def y_copy(src, dst, device):
        return pltpu.make_async_remote_copy(
            src_ref=src, dst_ref=dst, send_sem=ysem.at[0], recv_sem=ysem.at[1], device_id=device
        )

    def y_send(step, carry):
        to = lax.rem(hd + lax.div(nh, 2) + step, nh)
        y_copy(y_out, y_in.at[hd], {"head": to}).start()
        return carry

    lax.fori_loop(0, nh // 2, y_send, 0)
    lax.fori_loop(nh // 2 + 1, nh, y_send, 0)
    y_in[hd] = y_out[...]
    y_all = y_copy(y_in.at[pl.ds(0, nh - 1)], y_in.at[pl.ds(0, nh - 1)], {"head": lax.rem(hd + 1, nh)})
    y_all.wait_recv()
    sums = y_in[0]
    for i in range(1, nh):
        sums = sums + y_in[i]
    full = nh * width
    rinv = 1.0 / jnp.sqrt(sums[:, 0:rows] / full + EPSILON)
    coef = (sums[:, 256 : 256 + rows] * rinv / full) * rinv * rinv

    def to_column(lanes):
        return jnp.sum(jnp.where(row == col, lanes, 0.0), axis=1, keepdims=True)

    rinv_c = to_column(rinv)
    coef_c = to_column(coef)
    for h in range(heads):
        da_ref[:, hs(h)] = (gated[:, hs(h)] * rinv_c - att[:, hs(h)] * coef_c).astype(BF16)
        loc[1, hs(h)] = mm(lq_ref[:, hs(h)], da_ref[:, hs(h)], TN)
    pair2 = scan_pair(1)
    first2 = scan_out(1, pair2)

    og_ref[...] = (gg[...] * (att[...] * rinv_c)).astype(BF16)
    slope_q = silu_slope(q_ref[...].astype(F32))
    for h in range(heads):
        da, v, lk = da_ref[:, hs(h)], v_ref[:, hs(h)], lk_ref[:, hs(h)]
        dw = jnp.where(row >= col, mm(da, v, NT), 0.0).astype(BF16)
        glq = mm(dw, lk, NN) + mm(da, st1[hs(h)], NT)
        oq_ref[:, hs(h)] = (glq * slope_q[:, hs(h)]).astype(BF16)
    outs = [
        pltpu.make_async_copy(src, dst, out_sem.at[i])
        for i, (src, dst) in enumerate(((oq_ref, oq), (ok_ref, ok), (ov_ref, ov), (og_ref, og)))
    ]
    outs[0].start()
    outs[3].start()
    second2 = scan_back(1, first2, True)
    for h in range(heads):
        da, v, lq = da_ref[:, hs(h)], v_ref[:, hs(h)], lq_ref[:, hs(h)]
        dwt = jnp.where(col >= row, mm(v, da, NT), 0.0).astype(BF16)
        glk[:, hs(h)] = mm(dwt, lq, NN)
        gv[:, hs(h)] = mm(wt_ref[h], da, NN)
    gg[...] = silu_slope(k_ref[...].astype(F32))
    last2 = scan_end(1, second2, True, st2)
    for h in range(heads):
        s = st2[hs(h)]
        lk = glk[:, hs(h)] + mm(v_ref[:, hs(h)], s, NT)
        ok_ref[:, hs(h)] = (lk * gg[:, hs(h)]).astype(BF16)
        ov_ref[:, hs(h)] = (gv[:, hs(h)] + mm(lk_ref[:, hs(h)], s, NN)).astype(BF16)
    outs[1].start()
    outs[2].start()
    for sent in (pair1, first1, second1, last1, y_all, pair2, first2, second2, last2):
        sent.wait_send()
    for copy in outs:
        copy.wait()


def per_device(nx, nz, nh, queries, key_rows, value_rows, gate_rows, cotangent):
    rows, width = queries.shape
    heads = width // DH
    chips = nx * nz
    half = heads * DH // 2
    piece = half // chips
    block = pltpu.VMEM((rows, width), BF16)
    wide = pltpu.VMEM((rows, width), F32)
    pieces = pltpu.VMEM((2, chips, piece, DH), F32)
    halves = pltpu.VMEM((2, half, DH), F32)
    out = jax.ShapeDtypeStruct((rows, width), BF16)
    return pl.pallas_call(
        functools.partial(kernel, nx, nz, nh),
        out_shape=(out,) * 4,
        in_specs=[pl.BlockSpec(memory_space=pl.ANY)] * 5,
        out_specs=[pl.BlockSpec(memory_space=pl.ANY)] * 4,
        scratch_shapes=[
            block, block, block, block, block,
            block, block, block, pltpu.VMEM((heads, rows, rows), BF16),
            wide, wide, wide, wide, wide,
            pltpu.VMEM((heads * DH, DH), BF16), pltpu.VMEM((heads * DH, DH), BF16),
            pltpu.VMEM((2, heads * DH, DH), F32), halves, pieces, pieces, pieces, pieces, halves, halves,
            pltpu.VMEM((1, 512), F32), pltpu.VMEM((nh, 1, 512), F32),
            pltpu.SemaphoreType.DMA((5,)), pltpu.SemaphoreType.DMA((4,)),
            pltpu.SemaphoreType.DMA((2, 4)), pltpu.SemaphoreType.DMA((2, 4)), pltpu.SemaphoreType.DMA((2,)),
            block, block, block, block,
        ],
        compiler_params=pltpu.CompilerParams(collective_id=0, has_side_effects=True),
        name="linear_attention",
    )(queries, key_rows, value_rows, gate_rows, cotangent)


def solution(mesh):
    nh = mesh.shape["head"]
    nz = NZ
    nx = mesh.shape["ctx"] // (2 * nz)
    spec = P("ctx", "head")
    return jax.shard_map(
        functools.partial(per_device, nx, nz, nh),
        mesh=mesh, in_specs=(spec,) * 5, out_specs=(spec,) * 4, check_vma=False,
    )
```

```python
import functools

import jax
import jax.numpy as jnp
from jax import lax
from jax.experimental import pallas as pl
from jax.experimental.pallas import tpu as pltpu
from jax.sharding import PartitionSpec as P

H = 32
DH = 128
EPSILON = 1e-06
NZ = 8
F32 = jnp.float32
BF16 = jnp.bfloat16

NN = (((1,), (0,)), ((), ()))
NT = (((1,), (1,)), ((), ()))
TN = (((0,), (0,)), ((), ()))


def mm(a, b, dims):
    return lax.dot_general(a, b, dims, preferred_element_type=F32)


def silu_slope(x):
    sig = jax.nn.sigmoid(x)
    return sig * (1.0 + x * (1.0 - sig))


def kernel(
    nx, nz, nh,
    q_hbm, k_hbm, v_hbm, g_hbm, c_hbm,
    oq_ref, ok_ref, ov_ref, og_ref,
    q_ref, k_ref, v_ref, g_ref, c_ref,
    lq_ref, lk_ref, da_ref, wt_ref,
    att, gated, gg, glk, gv,
    st1, st2,
    loc, x_in, comb, a_in, p_out, e_in, f_out, f_in,
    y_out, y_in,
    in_sem, send_sem, recv_sem, ysem,
):
    rows, width = q_ref.shape
    heads = width // DH
    chips = nx * nz
    half = heads * DH // 2
    piece = half // chips
    me = lax.axis_index("ctx")
    hd = lax.axis_index("head")
    core = lax.rem(me, 2)
    chip = lax.div(me, 2)
    cx = lax.div(chip, nz)
    cz = lax.rem(chip, nz)
    partner = chip * 2 + (1 - core)

    ins = [
        pltpu.make_async_copy(src, dst, in_sem.at[i])
        for i, (src, dst) in enumerate(
            ((k_hbm, k_ref), (v_hbm, v_ref), (q_hbm, q_ref), (g_hbm, g_ref), (c_hbm, c_ref))
        )
    ]
    for copy in ins:
        copy.start()

    def far(i, n):
        odd = lax.rem(i, 2)
        return n // 2 + lax.div(i + 1, 2) * (1 - 2 * odd)

    def other_chip(step):
        dz = far(lax.div(step, nx), nz)
        dx = far(lax.rem(step, nx), nx)
        return lax.rem(cx + dx, nx) * nz + lax.rem(cz + dz, nz)

    barrier = pltpu.get_barrier_semaphore()

    def greet(step, carry):
        pl.semaphore_signal(barrier, inc=1, device_id={"ctx": other_chip(step) * 2 + core})
        return carry

    lax.fori_loop(0, chips - 1, greet, 0)

    def greet_head(step, carry):
        pl.semaphore_signal(barrier, inc=1, device_id={"head": lax.rem(hd + step, nh)})
        return carry

    lax.fori_loop(1, nh, greet_head, 0)
    pl.semaphore_signal(barrier, inc=1, device_id={"ctx": partner})

    def hs(h):
        return slice(h * DH, (h + 1) * DH)

    def remote(src, dst, scan, stage, device):
        return pltpu.make_async_remote_copy(
            src_ref=src,
            dst_ref=dst,
            send_sem=send_sem.at[scan, stage],
            recv_sem=recv_sem.at[scan, stage],
            device_id=device,
        )

    def scatter(src, dst, scan, stage):
        def one(step, carry):
            to = other_chip(step)
            remote(src.at[to], dst.at[chip], scan, stage, {"ctx": to * 2 + core}).start()
            return carry

        lax.fori_loop(0, chips - 1, one, 0)

    def scattered(src, dst, scan, stage):
        n = pl.ds(0, chips - 1)
        return remote(src.at[n], dst.at[n], scan, stage, {"ctx": partner})

    my_half = pl.ds(pl.multiple_of(core * half, half), half)
    other_half = pl.ds(pl.multiple_of((1 - core) * half, half), half)

    def scan_pair(scan):
        copy = remote(loc.at[scan, other_half], x_in.at[scan], scan, 0, {"ctx": partner})
        copy.start()
        return copy

    def scan_out(scan, pair):
        pair.wait_recv()
        both = loc[scan, my_half] + x_in[scan]
        comb[scan] = both.reshape(chips, piece, DH)
        scatter(comb.at[scan], a_in.at[scan], scan, 1)
        a_in[scan, chip] = comb[scan, chip]
        return scattered(comb.at[scan], a_in.at[scan], scan, 1)

    def scan_back(scan, first, reverse):
        first.wait_recv()
        total = jnp.zeros((piece, DH), F32)
        for i in range(chips):
            j = chips - 1 - i if reverse else i
            p_out[scan, j] = total
            total = total + a_in[scan, j]
        scatter(p_out.at[scan], e_in.at[scan], scan, 2)
        e_in[scan, chip] = p_out[scan, chip]
        return scattered(p_out.at[scan], e_in.at[scan], scan, 2)

    def scan_end(scan, second, reverse, state):
        second.wait_recv()
        later = 0 if reverse else 1
        mine = e_in[scan].reshape(half, DH)
        f_out[scan] = mine + jnp.where(core == later, 0.0, loc[scan, my_half])
        last = remote(f_out.at[scan], f_in.at[scan], scan, 3, {"ctx": partner})
        last.start()
        state[my_half] = (mine + jnp.where(core == later, x_in[scan], 0.0)).astype(BF16)
        last.wait_recv()
        state[other_half] = f_in[scan].astype(BF16)
        return last

    ins[0].wait()
    kf = k_ref[...].astype(F32)
    lk_ref[...] = jax.nn.silu(kf).astype(BF16)
    ins[1].wait()
    for h in range(heads):
        loc[0, hs(h)] = mm(lk_ref[:, hs(h)], v_ref[:, hs(h)], TN)
    pl.semaphore_wait(barrier, chips - 1 + 1 + nh - 1)
    pair1 = scan_pair(0)
    y_out[...] = jnp.zeros_like(y_out)
    first1 = scan_out(0, pair1)

    row = lax.broadcasted_iota(jnp.int32, (rows, rows), 0)
    col = lax.broadcasted_iota(jnp.int32, (rows, rows), 1)
    ins[2].wait()
    qf = q_ref[...].astype(F32)
    lq_ref[...] = jax.nn.silu(qf).astype(BF16)
    for h in range(heads):
        lq, lk, v = lq_ref[:, hs(h)], lk_ref[:, hs(h)], v_ref[:, hs(h)]
        w = jnp.where(row >= col, mm(lq, lk, NT), 0.0).astype(BF16)
        att[:, hs(h)] = mm(w, v, NN)
    second1 = scan_back(0, first1, False)
    ins[3].wait()
    ins[4].wait()
    sig = jax.nn.sigmoid(g_ref[...].astype(F32))
    gat = c_ref[...].astype(F32) * sig
    gated[...] = gat
    gg[...] = gat * (1.0 - sig)
    for h in range(heads):
        lq, lk = lq_ref[:, hs(h)], lk_ref[:, hs(h)]
        wt_ref[h] = jnp.where(col >= row, mm(lk, lq, NT), 0.0).astype(BF16)
    last1 = scan_end(0, second1, False, st1)

    sq = jnp.zeros((rows, DH), F32)
    dt = jnp.zeros((rows, DH), F32)
    for h in range(heads):
        a = att[:, hs(h)] + mm(lq_ref[:, hs(h)], st1[hs(h)], NN)
        att[:, hs(h)] = a
        sq = sq + a * a
        dt = dt + gated[:, hs(h)] * a

    def to_lanes(part):
        column = jnp.sum(part, axis=1, keepdims=True)
        return jnp.sum(jnp.where(row == col, column, 0.0), axis=0, keepdims=True)

    y_out[:, 0:rows] = to_lanes(sq)
    y_out[:, 256 : 256 + rows] = to_lanes(dt)

    def y_copy(src, dst, device):
        return pltpu.make_async_remote_copy(
            src_ref=src, dst_ref=dst, send_sem=ysem.at[0], recv_sem=ysem.at[1], device_id=device
        )

    def y_send(step, carry):
        to = lax.rem(hd + lax.div(nh, 2) + step, nh)
        y_copy(y_out, y_in.at[hd], {"head": to}).start()
        return carry

    lax.fori_loop(0, nh // 2, y_send, 0)
    lax.fori_loop(nh // 2 + 1, nh, y_send, 0)
    y_in[hd] = y_out[...]
    y_all = y_copy(y_in.at[pl.ds(0, nh - 1)], y_in.at[pl.ds(0, nh - 1)], {"head": lax.rem(hd + 1, nh)})
    y_all.wait_recv()
    sums = y_in[0]
    for i in range(1, nh):
        sums = sums + y_in[i]
    full = nh * width
    rinv = 1.0 / jnp.sqrt(sums[:, 0:rows] / full + EPSILON)
    coef = (sums[:, 256 : 256 + rows] * rinv / full) * rinv * rinv

    def to_column(lanes):
        return jnp.sum(jnp.where(row == col, lanes, 0.0), axis=1, keepdims=True)

    rinv_c = to_column(rinv)
    coef_c = to_column(coef)
    for h in range(heads):
        da_ref[:, hs(h)] = (gated[:, hs(h)] * rinv_c - att[:, hs(h)] * coef_c).astype(BF16)
        loc[1, hs(h)] = mm(lq_ref[:, hs(h)], da_ref[:, hs(h)], TN)
    pair2 = scan_pair(1)
    first2 = scan_out(1, pair2)

    og_ref[...] = (gg[...] * (att[...] * rinv_c)).astype(BF16)
    slope_q = silu_slope(q_ref[...].astype(F32))
    for h in range(heads):
        da, v, lk = da_ref[:, hs(h)], v_ref[:, hs(h)], lk_ref[:, hs(h)]
        dw = jnp.where(row >= col, mm(da, v, NT), 0.0).astype(BF16)
        glq = mm(dw, lk, NN) + mm(da, st1[hs(h)], NT)
        oq_ref[:, hs(h)] = (glq * slope_q[:, hs(h)]).astype(BF16)
    second2 = scan_back(1, first2, True)
    for h in range(heads):
        da, v, lq = da_ref[:, hs(h)], v_ref[:, hs(h)], lq_ref[:, hs(h)]
        dwt = jnp.where(col >= row, mm(v, da, NT), 0.0).astype(BF16)
        glk[:, hs(h)] = mm(dwt, lq, NN)
        gv[:, hs(h)] = mm(wt_ref[h], da, NN)
    gg[...] = silu_slope(k_ref[...].astype(F32))
    last2 = scan_end(1, second2, True, st2)
    for h in range(heads):
        s = st2[hs(h)]
        lk = glk[:, hs(h)] + mm(v_ref[:, hs(h)], s, NT)
        ok_ref[:, hs(h)] = (lk * gg[:, hs(h)]).astype(BF16)
        ov_ref[:, hs(h)] = (gv[:, hs(h)] + mm(lk_ref[:, hs(h)], s, NN)).astype(BF16)
    for sent in (pair1, first1, second1, last1, y_all, pair2, first2, second2, last2):
        sent.wait_send()


def write_out(a, b, c, d, oa, ob, oc, od, sem):
    copies = [
        pltpu.make_async_copy(src, dst, sem.at[i])
        for i, (src, dst) in enumerate(((a, oa), (b, ob), (c, oc), (d, od)))
    ]
    for copy in copies:
        copy.start()
    for copy in copies:
        copy.wait()


def per_device(nx, nz, nh, queries, key_rows, value_rows, gate_rows, cotangent):
    rows, width = queries.shape
    heads = width // DH
    chips = nx * nz
    half = heads * DH // 2
    piece = half // chips
    block = pltpu.VMEM((rows, width), BF16)
    wide = pltpu.VMEM((rows, width), F32)
    pieces = pltpu.VMEM((2, chips, piece, DH), F32)
    halves = pltpu.VMEM((2, half, DH), F32)
    out = jax.ShapeDtypeStruct((rows, width), BF16)
    outs = pl.pallas_call(
        functools.partial(kernel, nx, nz, nh),
        out_shape=(out,) * 4,
        in_specs=[pl.BlockSpec(memory_space=pltpu.HBM)] * 5,
        out_specs=[pl.BlockSpec(memory_space=pltpu.VMEM)] * 4,
        scratch_shapes=[
            block, block, block, block, block,
            block, block, block, pltpu.VMEM((heads, rows, rows), BF16),
            wide, wide, wide, wide, wide,
            pltpu.VMEM((heads * DH, DH), BF16), pltpu.VMEM((heads * DH, DH), BF16),
            pltpu.VMEM((2, heads * DH, DH), F32), halves, pieces, pieces, pieces, pieces, halves, halves,
            pltpu.VMEM((1, 512), F32), pltpu.VMEM((nh, 1, 512), F32),
            pltpu.SemaphoreType.DMA((5,)),
            pltpu.SemaphoreType.DMA((2, 4)), pltpu.SemaphoreType.DMA((2, 4)), pltpu.SemaphoreType.DMA((2,)),
        ],
        compiler_params=pltpu.CompilerParams(collective_id=0, has_side_effects=True, vmem_limit_bytes=16 << 20),
        name="linear_attention",
    )(*(pltpu.with_memory_space_constraint(a, pltpu.HBM) for a in (queries, key_rows, value_rows, gate_rows, cotangent)))
    return pl.pallas_call(
        write_out,
        out_shape=(out,) * 4,
        in_specs=[pl.BlockSpec(memory_space=pltpu.VMEM)] * 4,
        out_specs=[pl.BlockSpec(memory_space=pltpu.HBM)] * 4,
        scratch_shapes=[pltpu.SemaphoreType.DMA((4,))],
        compiler_params=pltpu.CompilerParams(vmem_limit_bytes=4 << 20),
        name="write_out",
    )(*outs)


def solution(mesh):
    nh = mesh.shape["head"]
    nz = NZ
    nx = mesh.shape["ctx"] // (2 * nz)
    spec = P("ctx", "head")
    return jax.shard_map(
        functools.partial(per_device, nx, nz, nh),
        mesh=mesh, in_specs=(spec,) * 5, out_specs=(spec,) * 4, check_vma=False,
    )
```

```python
import functools

import jax
import jax.numpy as jnp
from jax import lax
from jax.experimental import pallas as pl
from jax.experimental.pallas import tpu as pltpu
from jax.sharding import PartitionSpec as P

H = 32
DH = 128
EPSILON = 1e-06
NZ = 8
F32 = jnp.float32
BF16 = jnp.bfloat16

NN = (((1,), (0,)), ((), ()))
NT = (((1,), (1,)), ((), ()))
TN = (((0,), (0,)), ((), ()))


def mm(a, b, dims):
    return lax.dot_general(a, b, dims, preferred_element_type=F32)


def silu_slope(x):
    sig = jax.nn.sigmoid(x)
    return sig * (1.0 + x * (1.0 - sig))


def wrap(value, n):
    return jnp.where(value >= n, value - n, value)


def offsets(nx, nz):
    def away(d, n):
        return min(d, n - d)

    every = [(dx, dz) for dz in range(nz) for dx in range(nx) if dx or dz]
    return sorted(every, key=lambda o: (-away(o[0], nx) - away(o[1], nz), -away(o[1], nz)))


def kernel(
    nx, nz, nh,
    q_hbm, k_hbm, v_hbm, g_hbm, c_hbm,
    oq, ok, ov, og,
    q_ref, k_ref, v_ref, g_ref, c_ref,
    lq_ref, lk_ref, gat, gg,
    xo, xi, pq, pk, pv,
    att, wt, da, s1,
    loc, x_in, loc2, f_out, f_in,
    comb, a_in, p_out, e_in,
    ro, ri, mine,
    y_out, y_in,
    in_sem, send_sem, recv_sem,
):
    heads, rows, _ = q_ref.shape
    hh = heads // 2
    chips = nx * nz
    piece = hh * DH // chips
    me = lax.axis_index("ctx")
    hd = lax.axis_index("head")
    core = lax.rem(me, 2)
    chip = lax.div(me, 2)
    cx = lax.div(chip, nz)
    cz = lax.rem(chip, nz)
    partner = me + 1 - 2 * core
    own = core * hh
    other = hh - own

    def load(i, src, dst):
        copies = [
            pltpu.make_async_copy(src.at[:, pl.ds(h * DH, DH)], dst.at[h], in_sem.at[i, h])
            for h in range(heads)
        ]
        for copy in copies:
            copy.start()
        return copies

    def arrived(copies):
        for copy in copies:
            copy.wait()

    k_in, v_in = load(0, k_hbm, k_ref), load(1, v_hbm, v_ref)

    xs = [wrap(cx + d, nx) * nz for d in range(nx)]
    zs = [wrap(cz + d, nz) for d in range(nz)]
    targets = [xs[dx] + zs[dz] for dx, dz in offsets(nx, nz)]
    far_heads = sorted(range(1, nh), key=lambda d: -min(d, nh - d))
    head_targets = [wrap(hd + d, nh) for d in far_heads]

    barrier = pltpu.get_barrier_semaphore()
    for to in targets:
        pl.semaphore_signal(barrier, inc=1, device_id={"ctx": to * 2 + core})
    for to in head_targets:
        pl.semaphore_signal(barrier, inc=1, device_id={"head": to})
        pl.semaphore_signal(barrier, inc=1, device_id={"ctx": partner, "head": to})
    pl.semaphore_signal(barrier, inc=1, device_id={"ctx": partner})
    q_in, g_in, c_in = load(2, q_hbm, q_ref), load(3, g_hbm, g_ref), load(4, c_hbm, c_ref)

    def remote(src, dst, stage, device):
        return pltpu.make_async_remote_copy(
            src_ref=src,
            dst_ref=dst,
            send_sem=send_sem.at[stage],
            recv_sem=recv_sem.at[stage],
            device_id=device,
        )

    def scatter(src, dst, stage):
        for to in targets:
            remote(src.at[to], dst.at[chip], stage, {"ctx": to * 2 + core}).start()
        dst[chip] = src[chip]
        n = pl.ds(0, chips - 1)
        return remote(src.at[n], dst.at[n], stage, {"ctx": partner})

    def to_partner(src, dst, stage):
        copy = remote(src, dst, stage, {"ctx": partner})
        copy.start()
        return copy

    def scan_out(scan, total):
        comb[scan] = total.reshape(chips, piece, DH)
        return scatter(comb.at[scan], a_in.at[scan], 2 * scan)

    def scan_back(scan, first, reverse):
        first.wait_recv()
        total = jnp.zeros((piece, DH), F32)
        for i in range(chips):
            j = chips - 1 - i if reverse else i
            p_out[scan, j] = total
            total = total + a_in[scan, j]
        return scatter(p_out.at[scan], e_in.at[scan], 2 * scan + 1)

    arrived(k_in)
    arrived(v_in)

    def local(h):
        lk = jax.nn.silu(k_ref[h].astype(F32)).astype(BF16)
        lk_ref[h] = lk
        loc[h] = mm(lk, v_ref[h], TN)

    for i in range(hh):
        local(other + i)
    pl.semaphore_wait(barrier, chips - 1 + 2 * (nh - 1) + 1)
    pair = to_partner(loc.at[pl.ds(other, hh)], x_in, 4)
    for i in range(hh):
        local(own + i)
    pair.wait_recv()
    first1 = scan_out(0, loc[pl.ds(own, hh)] + x_in[...])

    arrived(q_in)
    arrived(g_in)
    arrived(c_in)

    def lift(h):
        lq_ref[h] = jax.nn.silu(q_ref[h].astype(F32)).astype(BF16)
        sig = jax.nn.sigmoid(g_ref[h].astype(F32))
        gated = c_ref[h].astype(F32) * sig
        gat[h] = gated
        gg[h] = gated * (1.0 - sig)

    for i in range(hh):
        h = other + i
        lift(h)
        xo[0, i] = lq_ref[h].astype(F32)
        xo[1, i] = lk_ref[h].astype(F32)
        xo[2, i] = v_ref[h].astype(F32)
        xo[3, i] = gat[h]
    swap = to_partner(xo, xi, 5)
    row = lax.broadcasted_iota(jnp.int32, (rows, rows), 0)
    col = lax.broadcasted_iota(jnp.int32, (rows, rows), 1)
    y_out[...] = jnp.zeros_like(y_out)

    def inner(side, i, lq, lk, v):
        w = jnp.where(row >= col, mm(lq, lk, NT), 0.0).astype(BF16)
        att[side, i] = mm(w, v, NN)
        wt[side, i] = jnp.where(col >= row, mm(lk, lq, NT), 0.0).astype(BF16)

    for i in range(hh):
        lift(own + i)
        inner(0, i, lq_ref[own + i], lk_ref[own + i], v_ref[own + i])
    second1 = scan_back(0, first1, False)
    swap.wait_recv()
    for i in range(hh):
        pq[i] = xi[0, i].astype(BF16)
        pk[i] = xi[1, i].astype(BF16)
        pv[i] = xi[2, i].astype(BF16)
        inner(1, i, pq[i], pk[i], pv[i])

    def operands(side, i):
        if side == 0:
            return lq_ref[own + i], lk_ref[own + i], v_ref[own + i]
        return pq[i], pk[i], pv[i]

    second1.wait_recv()
    state = e_in[0].reshape(hh, DH, DH)
    s1[0] = (state + jnp.where(core == 1, x_in[...], 0.0)).astype(BF16)
    s1[1] = (state + jnp.where(core == 0, loc[pl.ds(own, hh)], 0.0)).astype(BF16)
    parts = []
    for side in range(2):
        sq = jnp.zeros((rows, DH), F32)
        dt = jnp.zeros((rows, DH), F32)
        for i in range(hh):
            a = att[side, i] + mm(operands(side, i)[0], s1[side, i], NN)
            att[side, i] = a
            sq = sq + a * a
            dt = dt + (gat[own + i] if side == 0 else xi[3, i]) * a
        parts += [sq, dt]
    parts = jnp.concatenate(parts, axis=1)
    pick = lax.broadcasted_iota(jnp.int32, (8, 4 * DH), 0) == lax.div(
        lax.broadcasted_iota(jnp.int32, (8, 4 * DH), 1), DH
    )
    sums = lax.dot_general(
        jnp.where(pick, 1.0, 0.0), parts, NT, precision=lax.Precision.HIGHEST, preferred_element_type=F32
    )
    y_out[core, :, 0:rows] = sums[0:2]
    y_out[1 - core, :, 0:rows] = sums[2:4]
    slot = hd * 2 + core
    for to in head_targets:
        remote(y_out, y_in.at[slot], 6, {"head": to}).start()
        remote(y_out, y_in.at[slot], 6, {"ctx": partner, "head": to}).start()
    remote(y_out, y_in.at[slot], 6, {"ctx": partner}).start()
    y_in[slot] = y_out[...]
    n = pl.ds(0, 2 * nh - 1)
    y_all = remote(y_in.at[n], y_in.at[n], 6, {"ctx": partner})
    y_all.wait_recv()
    full = nh * heads * DH
    lanes = []
    for side in range(2):
        block = core if side == 0 else 1 - core
        tot = y_in[0, block]
        for j in range(1, 2 * nh):
            tot = tot + y_in[j, block]
        rinv = 1.0 / jnp.sqrt(tot[0:1] / full + EPSILON)
        lanes += [rinv, (tot[1:2] * rinv / full) * rinv * rinv]
    sub = lax.broadcasted_iota(jnp.int32, (8, lanes[0].shape[1]), 0)
    stacked = jnp.where(sub == 0, lanes[0], jnp.where(sub == 1, lanes[1], jnp.where(sub == 2, lanes[2], lanes[3])))
    columns = jnp.transpose(stacked)[0:rows]
    rinv_c = [columns[:, 0:1], columns[:, 2:3]]
    coef_c = [columns[:, 1:2], columns[:, 3:4]]
    for side in range(2):
        for i in range(hh):
            gated = gat[own + i] if side == 0 else xi[3, i]
            d = (gated * rinv_c[side] - att[side, i] * coef_c[side]).astype(BF16)
            da[side, i] = d
            loc2[side, i] = mm(operands(side, i)[0], d, TN)
    first2 = scan_out(1, loc2[0] + loc2[1])

    def inside(side, i):
        lq, lk, v = operands(side, i)
        d = da[side, i]
        dw = jnp.where(row >= col, mm(d, v, NT), 0.0).astype(BF16)
        dwt = jnp.where(col >= row, mm(v, d, NT), 0.0).astype(BF16)
        glq = mm(dw, lk, NN) + mm(d, s1[side, i], NT)
        return att[side, i] * rinv_c[side], glq, mm(dwt, lq, NN), mm(wt[side, i], d, NN)

    for i in range(hh):
        ro[0, i], ro[1, i], ro[2, i], ro[3, i] = inside(1, i)
    back = to_partner(ro, ri, 7)
    second2 = scan_back(1, first2, True)

    def settle(h, normed, glq):
        og[h] = (gg[h] * normed).astype(BF16)
        oq[h] = (glq * silu_slope(q_ref[h].astype(F32))).astype(BF16)
        gg[h] = silu_slope(k_ref[h].astype(F32))

    for i in range(hh):
        normed, glq, mine[0, i], mine[1, i] = inside(0, i)
        settle(own + i, normed, glq)
    back.wait_recv()
    for i in range(hh):
        settle(other + i, ri[0, i], ri[1, i])

    second2.wait_recv()
    state = e_in[1].reshape(hh, DH, DH)
    f_out[...] = state + jnp.where(core == 1, loc2[0], 0.0)
    last = to_partner(f_out, f_in, 8)

    def finish(h, s, glk, gv):
        s = s.astype(BF16)
        ok[h] = ((glk + mm(v_ref[h], s, NT)) * gg[h]).astype(BF16)
        ov[h] = (gv + mm(lk_ref[h], s, NN)).astype(BF16)

    state = state + jnp.where(core == 0, loc2[1], 0.0)
    for i in range(hh):
        finish(own + i, state[i], mine[0, i], mine[1, i])
    last.wait_recv()
    for i in range(hh):
        finish(other + i, f_in[i], ri[2, i], ri[3, i])
    for sent in (pair, first1, swap, second1, y_all, first2, back, second2, last):
        sent.wait_send()


def write_out(a, b, c, d, oa, ob, oc, od, sem):
    copies = [
        pltpu.make_async_copy(src.at[h], dst.at[:, pl.ds(h * DH, DH)], sem.at[i, h])
        for i, (src, dst) in enumerate(((a, oa), (b, ob), (c, oc), (d, od)))
        for h in range(a.shape[0])
    ]
    for copy in copies:
        copy.start()
    for copy in copies:
        copy.wait()


def per_device(nx, nz, nh, *args):
    rows, width = args[0].shape
    heads = width // DH
    hh = heads // 2
    chips = nx * nz
    piece = hh * DH // chips

    def vmem(dtype, *shape):
        return pltpu.VMEM(shape, dtype)

    low = vmem(BF16, heads, rows, DH)
    wide = vmem(F32, heads, rows, DH)
    low2 = vmem(BF16, hh, rows, DH)
    four = vmem(F32, 4, hh, rows, DH)
    half = vmem(F32, hh, DH, DH)
    pieces = vmem(F32, 2, chips, piece, DH)
    out = jax.ShapeDtypeStruct((heads, rows, DH), BF16)
    outs = pl.pallas_call(
        functools.partial(kernel, nx, nz, nh),
        out_shape=(out,) * 4,
        in_specs=[pl.BlockSpec(memory_space=pltpu.HBM)] * 5,
        out_specs=[pl.BlockSpec(memory_space=pltpu.VMEM)] * 4,
        scratch_shapes=[
            low, low, low, low, low,
            low, low, wide, wide,
            four, four, low2, low2, low2,
            vmem(F32, 2, hh, rows, DH), vmem(BF16, 2, hh, rows, rows), vmem(BF16, 2, hh, rows, DH), vmem(BF16, 2, hh, DH, DH),
            vmem(F32, heads, DH, DH), half, vmem(F32, 2, hh, DH, DH), half, half,
            pieces, pieces, pieces, pieces,
            four, four, vmem(F32, 2, hh, rows, DH),
            vmem(F32, 2, 2, 256), vmem(F32, 2 * nh, 2, 2, 256),
            pltpu.SemaphoreType.DMA((5, heads)), pltpu.SemaphoreType.DMA((9,)), pltpu.SemaphoreType.DMA((9,)),
        ],
        compiler_params=pltpu.CompilerParams(collective_id=0, has_side_effects=True, vmem_limit_bytes=32 << 20),
        name="linear_attention",
    )(*(pltpu.with_memory_space_constraint(a, pltpu.HBM) for a in args))
    flat = jax.ShapeDtypeStruct((rows, width), BF16)
    return pl.pallas_call(
        write_out,
        out_shape=(flat,) * 4,
        in_specs=[pl.BlockSpec(memory_space=pltpu.VMEM)] * 4,
        out_specs=[pl.BlockSpec(memory_space=pltpu.HBM)] * 4,
        scratch_shapes=[pltpu.SemaphoreType.DMA((4, heads))],
        compiler_params=pltpu.CompilerParams(vmem_limit_bytes=4 << 20),
        name="write_out",
    )(*outs)


def solution(mesh):
    nh = mesh.shape["head"]
    nz = NZ
    nx = mesh.shape["ctx"] // (2 * nz)
    spec = P("ctx", "head")
    return jax.shard_map(
        functools.partial(per_device, nx, nz, nh),
        mesh=mesh, in_specs=(spec,) * 5, out_specs=(spec,) * 4, check_vma=False,
    )
```

```python
import functools

import jax
import jax.numpy as jnp
from jax import lax
from jax.experimental import pallas as pl
from jax.experimental.pallas import tpu as pltpu
from jax.sharding import PartitionSpec as P

H = 32
DH = 128
EPSILON = 1e-06
NZ = 8
F32 = jnp.float32
BF16 = jnp.bfloat16

NN = (((1,), (0,)), ((), ()))
NT = (((1,), (1,)), ((), ()))
TN = (((0,), (0,)), ((), ()))


def mm(a, b, dims):
    return lax.dot_general(a, b, dims, preferred_element_type=F32)


def silu_slope(x):
    sig = jax.nn.sigmoid(x)
    return sig * (1.0 + x * (1.0 - sig))


def wrap(value, n):
    return jnp.where(value >= n, value - n, value)


def offsets(nx, nz):
    def away(d, n):
        return min(d, n - d)

    every = [(dx, dz) for dz in range(nz) for dx in range(nx) if dx or dz]
    return sorted(every, key=lambda o: (-away(o[0], nx) - away(o[1], nz), -away(o[1], nz)))


def kernel(
    nx, nz, nh,
    q_hbm, k_hbm, v_hbm, g_hbm, c_hbm,
    oq, og, v_ref, lk_ref, glk, gv, sk, s2,
    q_ref, k_ref, g_ref, c_ref,
    lq_ref, gat, gg,
    xo, xi, pq, pk, pv,
    att, wt, da, s1, lqt,
    loc, x_in, loc2, f_out, f_in, l_in,
    comb, a_in, p_out, e_in, e_far,
    ro, ri,
    y_out, y_in,
    in_sem, send_sem, recv_sem,
):
    heads, rows, _ = q_ref.shape
    hh = heads // 2
    chips = nx * nz
    piece = hh * DH // chips
    me = lax.axis_index("ctx")
    hd = lax.axis_index("head")
    core = lax.rem(me, 2)
    chip = lax.div(me, 2)
    cx = lax.div(chip, nz)
    cz = lax.rem(chip, nz)
    partner = me + 1 - 2 * core
    own = core * hh
    other = hh - own

    def load(i, src, dst):
        copies = [
            pltpu.make_async_copy(src.at[:, pl.ds(h * DH, DH)], dst.at[h], in_sem.at[i, h])
            for h in range(heads)
        ]
        for copy in copies:
            copy.start()
        return copies

    def arrived(copies):
        for copy in copies:
            copy.wait()

    xs = [wrap(cx + d, nx) * nz for d in range(nx)]
    zs = [wrap(cz + d, nz) for d in range(nz)]
    targets = [xs[dx] + zs[dz] for dx, dz in offsets(nx, nz)]
    far_heads = sorted(range(1, nh), key=lambda d: -min(d, nh - d))
    head_targets = [wrap(hd + d, nh) for d in far_heads]

    barrier = pltpu.get_barrier_semaphore()
    for to in targets:
        pl.semaphore_signal(barrier, inc=1, device_id={"ctx": to * 2 + core})
    for to in head_targets:
        pl.semaphore_signal(barrier, inc=1, device_id={"head": to})
        pl.semaphore_signal(barrier, inc=1, device_id={"ctx": partner, "head": to})
    pl.semaphore_signal(barrier, inc=1, device_id={"ctx": partner})
    k_in, v_in = load(0, k_hbm, k_ref), load(1, v_hbm, v_ref)
    q_in, g_in, c_in = load(2, q_hbm, q_ref), load(3, g_hbm, g_ref), load(4, c_hbm, c_ref)

    def remote(src, dst, stage, device):
        return pltpu.make_async_remote_copy(
            src_ref=src,
            dst_ref=dst,
            send_sem=send_sem.at[stage],
            recv_sem=recv_sem.at[stage],
            device_id=device,
        )

    def scatter(src, dst, stage):
        for to in targets:
            remote(src.at[to], dst.at[chip], stage, {"ctx": to * 2 + core}).start()
        dst[chip] = src[chip]
        n = pl.ds(0, chips - 1)
        return remote(src.at[n], dst.at[n], stage, {"ctx": partner})

    def to_partner(src, dst, stage):
        copy = remote(src, dst, stage, {"ctx": partner})
        copy.start()
        return copy

    def scan_out(scan, total):
        comb[scan] = total.reshape(chips, piece, DH)
        return scatter(comb.at[scan], a_in.at[scan], 2 * scan)

    def scan_back(scan, first, reverse):
        first.wait_recv()
        total = jnp.zeros((piece, DH), F32)
        for i in range(chips):
            j = chips - 1 - i if reverse else i
            p_out[scan, j] = total
            total = total + a_in[scan, j]
        extra = None
        if reverse:
            extra = remote(p_out.at[scan, 0], e_far.at[chip], 9, {"ctx": 1 - core})
            extra.start()
        return scatter(p_out.at[scan], e_in.at[scan], 2 * scan + 1), extra

    arrived(k_in)
    arrived(v_in)

    def local(h):
        lk = jax.nn.silu(k_ref[h].astype(F32)).astype(BF16)
        lk_ref[h] = lk
        loc[h] = mm(lk, v_ref[h], TN)

    for i in range(hh):
        local(other + i)
    pl.semaphore_wait(barrier, chips - 1 + 2 * (nh - 1) + 1)
    pair = to_partner(loc.at[pl.ds(other, hh)], x_in, 4)
    for i in range(hh):
        local(own + i)
    pair.wait_recv()
    first1 = scan_out(0, loc[pl.ds(own, hh)] + x_in[...])

    arrived(q_in)
    arrived(g_in)
    arrived(c_in)

    def lift(h):
        lq_ref[h] = jax.nn.silu(q_ref[h].astype(F32)).astype(BF16)
        sig = jax.nn.sigmoid(g_ref[h].astype(F32))
        gated = c_ref[h].astype(F32) * sig
        gat[h] = gated
        gg[h] = gated * (1.0 - sig)

    for i in range(hh):
        h = other + i
        lift(h)
        xo[0, i] = lq_ref[h].astype(F32)
        xo[1, i] = lk_ref[h].astype(F32)
        xo[2, i] = v_ref[h].astype(F32)
        xo[3, i] = gat[h]
    swap = to_partner(xo, xi, 5)
    row = lax.broadcasted_iota(jnp.int32, (rows, rows), 0)
    col = lax.broadcasted_iota(jnp.int32, (rows, rows), 1)

    def inner(side, i, lq, lk, v):
        w = jnp.where(row >= col, mm(lq, lk, NT), 0.0).astype(BF16)
        att[side, i] = mm(w, v, NN)
        wt[side, i] = jnp.where(col >= row, mm(lk, lq, NT), 0.0).astype(BF16)
        lqt[side, i] = jnp.transpose(lq)

    for i in range(hh):
        lift(own + i)
        inner(0, i, lq_ref[own + i], lk_ref[own + i], v_ref[own + i])
    second1, _ = scan_back(0, first1, False)
    swap.wait_recv()
    for i in range(hh):
        pq[i] = xi[0, i].astype(BF16)
        pk[i] = xi[1, i].astype(BF16)
        pv[i] = xi[2, i].astype(BF16)
        inner(1, i, pq[i], pk[i], pv[i])

    def operands(side, i):
        if side == 0:
            return lq_ref[own + i], lk_ref[own + i], v_ref[own + i]
        return pq[i], pk[i], pv[i]

    second1.wait_recv()
    state = e_in[0].reshape(hh, DH, DH)
    s1[0] = (state + jnp.where(core == 1, x_in[...], 0.0)).astype(BF16)
    s1[1] = (state + jnp.where(core == 0, loc[pl.ds(own, hh)], 0.0)).astype(BF16)
    parts = []
    for side in range(2):
        sq = jnp.zeros((rows, DH), F32)
        dt = jnp.zeros((rows, DH), F32)
        for i in range(hh):
            a = att[side, i] + mm(operands(side, i)[0], s1[side, i], NN)
            att[side, i] = a
            sq = sq + a * a
            dt = dt + (gat[own + i] if side == 0 else xi[3, i]) * a
        parts += [sq, dt]
    lane = lax.broadcasted_iota(jnp.int32, (rows, DH), 1)
    spread = jnp.zeros((rows, DH), F32)
    for at, part in enumerate(parts):
        spread = jnp.where(lane == at, jnp.sum(part, axis=1, keepdims=True), spread)
    sums = jnp.transpose(spread)
    y_out[core] = jnp.concatenate([sums[0:1], sums[1:2]], axis=1)
    y_out[1 - core] = jnp.concatenate([sums[2:3], sums[3:4]], axis=1)
    slot = hd * 2 + core
    for to in head_targets:
        remote(y_out, y_in.at[slot], 6, {"head": to}).start()
        remote(y_out, y_in.at[slot], 6, {"ctx": partner, "head": to}).start()
    remote(y_out, y_in.at[slot], 6, {"ctx": partner}).start()
    y_in[slot] = y_out[...]
    n = pl.ds(0, 2 * nh - 1)
    y_all = remote(y_in.at[n], y_in.at[n], 6, {"ctx": partner})
    y_all.wait_recv()
    full = nh * heads * DH
    lanes = []
    for side in range(2):
        block = core if side == 0 else 1 - core
        tot = y_in[0, block]
        for j in range(1, 2 * nh):
            tot = tot + y_in[j, block]
        rinv = 1.0 / jnp.sqrt(tot[:, 0:rows] / full + EPSILON)
        lanes += [rinv, (tot[:, rows : 2 * rows] * rinv / full) * rinv * rinv]
    sub = lax.broadcasted_iota(jnp.int32, (8, lanes[0].shape[1]), 0)
    stacked = jnp.where(sub == 0, lanes[0], jnp.where(sub == 1, lanes[1], jnp.where(sub == 2, lanes[2], lanes[3])))
    columns = jnp.transpose(stacked)
    rinv_c = [columns[:, 0:1], columns[:, 2:3]]
    coef_c = [columns[:, 1:2], columns[:, 3:4]]
    for side in range(2):
        for i in range(hh):
            gated = gat[own + i] if side == 0 else xi[3, i]
            d = (gated * rinv_c[side] - att[side, i] * coef_c[side]).astype(BF16)
            da[side, i] = d
            loc2[side, i] = mm(lqt[side, i], d, NN)
    first2 = scan_out(1, loc2[0] + loc2[1])

    @pl.when(chip == 0)
    def _():
        to_partner(loc2.at[0], l_in, 10)

    def inside(side, i):
        lq, lk, v = operands(side, i)
        d = da[side, i]
        dw = jnp.where(row >= col, mm(d, v, NT), 0.0).astype(BF16)
        dwt = jnp.where(col >= row, mm(v, d, NT), 0.0).astype(BF16)
        glq = mm(dw, lk, NN) + mm(d, s1[side, i], NT)
        return att[side, i] * rinv_c[side], glq, mm(dwt, lq, NN), mm(wt[side, i], d, NN)

    for i in range(hh):
        ro[0, i], ro[1, i], ro[2, i], ro[3, i] = inside(1, i)
    back = to_partner(ro, ri, 7)
    second2, extra = scan_back(1, first2, True)

    def settle(h, normed, glq):
        og[h] = (gg[h] * normed).astype(BF16)
        oq[h] = (glq * silu_slope(q_ref[h].astype(F32))).astype(BF16)
        sk[h] = silu_slope(k_ref[h].astype(F32))

    for i in range(hh):
        normed, glq, glk[own + i], gv[own + i] = inside(0, i)
        settle(own + i, normed, glq)
    back.wait_recv()
    for i in range(hh):
        settle(other + i, ri[0, i], ri[1, i])
        glk[other + i] = ri[2, i]
        gv[other + i] = ri[3, i]

    second2.wait_recv()
    state = e_in[1].reshape(hh, DH, DH)
    s2[pl.ds(own, hh)] = (state + jnp.where(core == 0, loc2[1], 0.0)).astype(BF16)

    @pl.when(chip != 0)
    def _():
        f_out[...] = state + jnp.where(core == 1, loc2[0], 0.0)
        last = to_partner(f_out, f_in, 8)
        last.wait_recv()
        s2[pl.ds(other, hh)] = f_in[...].astype(BF16)
        last.wait_send()

    @pl.when(chip == 0)
    def _():
        remote(loc2.at[0], l_in, 10, {"ctx": partner}).wait()
        remote(e_far, e_far, 9, {"ctx": partner}).wait_recv()
        far = e_far[...].reshape(hh, DH, DH)
        s2[pl.ds(other, hh)] = (far + jnp.where(core == 0, l_in[...], 0.0)).astype(BF16)

    for sent in (pair, first1, swap, second1, y_all, first2, back, second2, extra):
        sent.wait_send()


def finish(oq, og, v, lk, glk, gv, sk, s2, dq, dk, dv, dg, ok, ov, sem):
    heads = oq.shape[0]

    def put(i, src, dst, h):
        copy = pltpu.make_async_copy(src.at[h], dst.at[:, pl.ds(h * DH, DH)], sem.at[i, h])
        copy.start()
        return copy

    copies = [put(0, oq, dq, h) for h in range(heads)] + [put(1, og, dg, h) for h in range(heads)]
    for h in range(heads):
        ok[h] = ((glk[h] + mm(v[h], s2[h], NT)) * sk[h]).astype(BF16)
        copies.append(put(2, ok, dk, h))
        ov[h] = (gv[h] + mm(lk[h], s2[h], NN)).astype(BF16)
        copies.append(put(3, ov, dv, h))
    for copy in copies:
        copy.wait()


def per_device(nx, nz, nh, *args):
    rows, width = args[0].shape
    heads = width // DH
    hh = heads // 2
    chips = nx * nz
    piece = hh * DH // chips

    def vmem(dtype, *shape):
        return pltpu.VMEM(shape, dtype)

    low = vmem(BF16, heads, rows, DH)
    wide = vmem(F32, heads, rows, DH)
    low2 = vmem(BF16, hh, rows, DH)
    four = vmem(F32, 4, hh, rows, DH)
    half = vmem(F32, hh, DH, DH)
    pieces = vmem(F32, 2, chips, piece, DH)
    def shape(dtype, *dims):
        return jax.ShapeDtypeStruct(dims, dtype)

    out, out_wide = shape(BF16, heads, rows, DH), shape(F32, heads, rows, DH)
    outs = pl.pallas_call(
        functools.partial(kernel, nx, nz, nh),
        out_shape=(out, out, out, out, out_wide, out_wide, out_wide, shape(BF16, heads, DH, DH)),
        in_specs=[pl.BlockSpec(memory_space=pltpu.HBM)] * 5,
        out_specs=[pl.BlockSpec(memory_space=pltpu.VMEM)] * 8,
        scratch_shapes=[
            low, low, low, low,
            low, wide, wide,
            four, four, low2, low2, low2,
            vmem(F32, 2, hh, rows, DH), vmem(BF16, 2, hh, rows, rows), vmem(BF16, 2, hh, rows, DH),
            vmem(BF16, 2, hh, DH, DH), vmem(BF16, 2, hh, DH, rows),
            vmem(F32, heads, DH, DH), half, vmem(F32, 2, hh, DH, DH), half, half, half,
            pieces, pieces, pieces, pieces, vmem(F32, chips, piece, DH),
            four, four,
            vmem(F32, 2, 1, 2 * rows), vmem(F32, 2 * nh, 2, 1, 2 * rows),
            pltpu.SemaphoreType.DMA((5, heads)), pltpu.SemaphoreType.DMA((11,)), pltpu.SemaphoreType.DMA((11,)),
        ],
        compiler_params=pltpu.CompilerParams(collective_id=0, has_side_effects=True, vmem_limit_bytes=32 << 20),
        name="linear_attention",
    )(*(pltpu.with_memory_space_constraint(a, pltpu.HBM) for a in args))
    return pl.pallas_call(
        finish,
        out_shape=(shape(BF16, rows, width),) * 4,
        in_specs=[pl.BlockSpec(memory_space=pltpu.VMEM)] * 8,
        out_specs=[pl.BlockSpec(memory_space=pltpu.HBM)] * 4,
        scratch_shapes=[low, low, pltpu.SemaphoreType.DMA((4, heads))],
        compiler_params=pltpu.CompilerParams(vmem_limit_bytes=8 << 20),
        name="finish",
    )(*outs)


def solution(mesh):
    nh = mesh.shape["head"]
    nz = NZ
    nx = mesh.shape["ctx"] // (2 * nz)
    spec = P("ctx", "head")
    return jax.shard_map(
        functools.partial(per_device, nx, nz, nh),
        mesh=mesh, in_specs=(spec,) * 5, out_specs=(spec,) * 4, check_vma=False,
    )
```

```python
import functools

import jax
import jax.numpy as jnp
from jax import lax
from jax.experimental import pallas as pl
from jax.experimental.pallas import tpu as pltpu
from jax.sharding import PartitionSpec as P

H = 32
DH = 128
EPSILON = 1e-06
NZ = 8
F32 = jnp.float32
BF16 = jnp.bfloat16

NN = (((1,), (0,)), ((), ()))
NT = (((1,), (1,)), ((), ()))
TN = (((0,), (0,)), ((), ()))


def mm(a, b, dims):
    return lax.dot_general(a, b, dims, preferred_element_type=F32)


def silu_slope(x):
    sig = jax.nn.sigmoid(x)
    return sig * (1.0 + x * (1.0 - sig))


def wrap(value, n):
    return jnp.where(value >= n, value - n, value)


def offsets(nx, nz):
    def away(d, n):
        return min(d, n - d)

    every = [(dx, dz) for dz in range(nz) for dx in range(nx) if dx or dz]
    return sorted(every, key=lambda o: (-away(o[0], nx) - away(o[1], nz), -away(o[1], nz)))


def kernel(
    nx, nz, nh,
    q_hbm, k_hbm, v_hbm, g_hbm, c_hbm,
    oq, og, v_ref, lk_ref, glk, gv, sk, s2,
    q_ref, k_ref, g_ref, c_ref,
    lq_ref, gat, gg,
    xo, xi, pq, pk, pv,
    att, wt, da, s1, lqt,
    loc, x_in, loc2, f_out, f_in, l_in,
    comb, a_in, p_out, e_in, e_far,
    ro, ri,
    y_out, y_in,
    in_sem, send_sem, recv_sem,
):
    heads, rows, _ = q_ref.shape
    hh = heads // 2
    chips = nx * nz
    piece = hh * DH // chips
    me = lax.axis_index("ctx")
    hd = lax.axis_index("head")
    core = lax.rem(me, 2)
    chip = lax.div(me, 2)
    cx = lax.div(chip, nz)
    cz = lax.rem(chip, nz)
    partner = me + 1 - 2 * core
    own = core * hh
    other = hh - own

    def load(i, src, dst):
        copies = [
            pltpu.make_async_copy(src.at[:, pl.ds(h * DH, DH)], dst.at[h], in_sem.at[i, h])
            for h in range(heads)
        ]
        for copy in copies:
            copy.start()
        return copies

    def arrived(copies):
        for copy in copies:
            copy.wait()

    xs = [wrap(cx + d, nx) * nz for d in range(nx)]
    zs = [wrap(cz + d, nz) for d in range(nz)]
    targets = [xs[dx] + zs[dz] for dx, dz in offsets(nx, nz)]
    far_heads = sorted(range(1, nh), key=lambda d: -min(d, nh - d))
    head_targets = [wrap(hd + d, nh) for d in far_heads]

    barrier = pltpu.get_barrier_semaphore()

    def greet(device):
        pl.semaphore_signal(barrier, inc=1, device_id=device)

    @pl.when(core == 0)
    def _():
        greet({"ctx": partner})

    for to in targets[:6]:
        greet({"ctx": to * 2})
    k_in, v_in = load(0, k_hbm, k_ref), load(1, v_hbm, v_ref)
    for to in targets[6:]:
        greet({"ctx": to * 2})
    for to in head_targets:
        greet({"ctx": chip * 2, "head": to})
    q_in, g_in, c_in = load(2, q_hbm, q_ref), load(3, g_hbm, g_ref), load(4, c_hbm, c_ref)

    def remote(src, dst, stage, device):
        return pltpu.make_async_remote_copy(
            src_ref=src,
            dst_ref=dst,
            send_sem=send_sem.at[stage],
            recv_sem=recv_sem.at[stage],
            device_id=device,
        )

    def scatter(src, dst, stage):
        for to in targets:
            remote(src.at[to], dst.at[chip], stage, {"ctx": to * 2 + core}).start()
        dst[chip] = src[chip]
        n = pl.ds(0, chips - 1)
        return remote(src.at[n], dst.at[n], stage, {"ctx": partner})

    def to_partner(src, dst, stage):
        copy = remote(src, dst, stage, {"ctx": partner})
        copy.start()
        return copy

    def scan_out(scan, total):
        comb[scan] = total.reshape(chips, piece, DH)
        return scatter(comb.at[scan], a_in.at[scan], 2 * scan)

    def scan_back(scan, first, reverse):
        first.wait_recv()
        total = jnp.zeros((piece, DH), F32)
        for i in range(chips):
            j = chips - 1 - i if reverse else i
            p_out[scan, j] = total
            total = total + a_in[scan, j]
        extra = None
        if reverse:
            extra = remote(p_out.at[scan, 0], e_far.at[chip], 9, {"ctx": 1 - core})
            extra.start()
        return scatter(p_out.at[scan], e_in.at[scan], 2 * scan + 1), extra

    arrived(k_in)
    arrived(v_in)

    def local(h):
        lk = jax.nn.silu(k_ref[h].astype(F32)).astype(BF16)
        lk_ref[h] = lk
        loc[h] = mm(lk, v_ref[h], TN)

    pair = remote(loc.at[pl.ds(other, hh)], x_in, 4, {"ctx": partner})
    for i in range(hh):
        local(other + i)

    @pl.when(core == 1)
    def _():
        pl.semaphore_wait(barrier, 1)

    @pl.when(core == 0)
    def _():
        pair.wait_recv()

    pair.start()
    for i in range(hh):
        local(own + i)

    @pl.when(core == 1)
    def _():
        pair.wait_recv()

    @pl.when(core == 0)
    def _():
        pl.semaphore_wait(barrier, 2 * (chips - 1) + 2 * (nh - 1))
        greet({"ctx": partner})

    @pl.when(core == 1)
    def _():
        pl.semaphore_wait(barrier, 1)

    first1 = scan_out(0, loc[pl.ds(own, hh)] + x_in[...])

    arrived(q_in)
    arrived(g_in)
    arrived(c_in)

    def lift(h):
        lq_ref[h] = jax.nn.silu(q_ref[h].astype(F32)).astype(BF16)
        sig = jax.nn.sigmoid(g_ref[h].astype(F32))
        gated = c_ref[h].astype(F32) * sig
        gat[h] = gated
        gg[h] = gated * (1.0 - sig)

    for i in range(hh):
        h = other + i
        lift(h)
        xo[0, i] = lq_ref[h].astype(F32)
        xo[1, i] = lk_ref[h].astype(F32)
        xo[2, i] = v_ref[h].astype(F32)
        xo[3, i] = gat[h]
    swap = to_partner(xo, xi, 5)
    row = lax.broadcasted_iota(jnp.int32, (rows, rows), 0)
    col = lax.broadcasted_iota(jnp.int32, (rows, rows), 1)

    def inner(side, i, lq, lk, v):
        w = jnp.where(row >= col, mm(lq, lk, NT), 0.0).astype(BF16)
        att[side, i] = mm(w, v, NN)
        wt[side, i] = jnp.where(col >= row, mm(lk, lq, NT), 0.0).astype(BF16)
        lqt[side, i] = jnp.transpose(lq)

    for i in range(hh):
        lift(own + i)
        inner(0, i, lq_ref[own + i], lk_ref[own + i], v_ref[own + i])
    second1, _ = scan_back(0, first1, False)
    swap.wait_recv()
    for i in range(hh):
        pq[i] = xi[0, i].astype(BF16)
        pk[i] = xi[1, i].astype(BF16)
        pv[i] = xi[2, i].astype(BF16)
        inner(1, i, pq[i], pk[i], pv[i])

    def operands(side, i):
        if side == 0:
            return lq_ref[own + i], lk_ref[own + i], v_ref[own + i]
        return pq[i], pk[i], pv[i]

    second1.wait_recv()
    state = e_in[0].reshape(hh, DH, DH)
    s1[0] = (state + jnp.where(core == 1, x_in[...], 0.0)).astype(BF16)
    s1[1] = (state + jnp.where(core == 0, loc[pl.ds(own, hh)], 0.0)).astype(BF16)
    parts = []
    for side in range(2):
        sq = jnp.zeros((rows, DH), F32)
        dt = jnp.zeros((rows, DH), F32)
        for i in range(hh):
            a = att[side, i] + mm(operands(side, i)[0], s1[side, i], NN)
            att[side, i] = a
            sq = sq + a * a
            dt = dt + (gat[own + i] if side == 0 else xi[3, i]) * a
        parts += [sq, dt]
    lane = lax.broadcasted_iota(jnp.int32, (rows, DH), 1)
    spread = jnp.zeros((rows, DH), F32)
    for at, part in enumerate(parts):
        spread = jnp.where(lane == at, jnp.sum(part, axis=1, keepdims=True), spread)
    sums = jnp.transpose(spread)
    y_out[core] = jnp.concatenate([sums[0:1], sums[1:2]], axis=1)
    y_out[1 - core] = jnp.concatenate([sums[2:3], sums[3:4]], axis=1)
    slot = hd * 2 + core
    for to in head_targets:
        remote(y_out, y_in.at[slot], 6, {"head": to}).start()
        remote(y_out, y_in.at[slot], 6, {"ctx": partner, "head": to}).start()
    remote(y_out, y_in.at[slot], 6, {"ctx": partner}).start()
    y_in[slot] = y_out[...]
    n = pl.ds(0, 2 * nh - 1)
    y_all = remote(y_in.at[n], y_in.at[n], 6, {"ctx": partner})
    y_all.wait_recv()
    full = nh * heads * DH
    lanes = []
    for side in range(2):
        block = core if side == 0 else 1 - core
        tot = y_in[0, block]
        for j in range(1, 2 * nh):
            tot = tot + y_in[j, block]
        rinv = 1.0 / jnp.sqrt(tot[:, 0:rows] / full + EPSILON)
        lanes += [rinv, (tot[:, rows : 2 * rows] * rinv / full) * rinv * rinv]
    sub = lax.broadcasted_iota(jnp.int32, (8, lanes[0].shape[1]), 0)
    stacked = jnp.where(sub == 0, lanes[0], jnp.where(sub == 1, lanes[1], jnp.where(sub == 2, lanes[2], lanes[3])))
    columns = jnp.transpose(stacked)
    rinv_c = [columns[:, 0:1], columns[:, 2:3]]
    coef_c = [columns[:, 1:2], columns[:, 3:4]]
    for side in range(2):
        for i in range(hh):
            gated = gat[own + i] if side == 0 else xi[3, i]
            d = (gated * rinv_c[side] - att[side, i] * coef_c[side]).astype(BF16)
            da[side, i] = d
            loc2[side, i] = mm(lqt[side, i], d, NN)
    first2 = scan_out(1, loc2[0] + loc2[1])

    @pl.when(chip == 0)
    def _():
        to_partner(loc2.at[0], l_in, 10)

    def inside(side, i):
        lq, lk, v = operands(side, i)
        d = da[side, i]
        dw = jnp.where(row >= col, mm(d, v, NT), 0.0).astype(BF16)
        dwt = jnp.where(col >= row, mm(v, d, NT), 0.0).astype(BF16)
        glq = mm(dw, lk, NN) + mm(d, s1[side, i], NT)
        return att[side, i] * rinv_c[side], glq, mm(dwt, lq, NN), mm(wt[side, i], d, NN)

    for i in range(hh):
        ro[0, i], ro[1, i], ro[2, i], ro[3, i] = inside(1, i)
    back = to_partner(ro, ri, 7)
    second2, extra = scan_back(1, first2, True)

    def settle(h, normed, glq):
        og[h] = (gg[h] * normed).astype(BF16)
        oq[h] = (glq * silu_slope(q_ref[h].astype(F32))).astype(BF16)
        sk[h] = silu_slope(k_ref[h].astype(F32))

    for i in range(hh):
        normed, glq, glk[own + i], gv[own + i] = inside(0, i)
        settle(own + i, normed, glq)
    back.wait_recv()
    for i in range(hh):
        settle(other + i, ri[0, i], ri[1, i])
        glk[other + i] = ri[2, i]
        gv[other + i] = ri[3, i]

    second2.wait_recv()
    state = e_in[1].reshape(hh, DH, DH)
    s2[pl.ds(own, hh)] = (state + jnp.where(core == 0, loc2[1], 0.0)).astype(BF16)

    @pl.when(chip != 0)
    def _():
        f_out[...] = state + jnp.where(core == 1, loc2[0], 0.0)
        last = to_partner(f_out, f_in, 8)
        last.wait_recv()
        s2[pl.ds(other, hh)] = f_in[...].astype(BF16)
        last.wait_send()

    @pl.when(chip == 0)
    def _():
        remote(loc2.at[0], l_in, 10, {"ctx": partner}).wait()
        remote(e_far, e_far, 9, {"ctx": partner}).wait_recv()
        far = e_far[...].reshape(hh, DH, DH)
        s2[pl.ds(other, hh)] = (far + jnp.where(core == 0, l_in[...], 0.0)).astype(BF16)

    for sent in (pair, first1, swap, second1, y_all, first2, back, second2, extra):
        sent.wait_send()


def finish(oq, og, v, lk, glk, gv, sk, s2, dq, dk, dv, dg, ok, ov, sem):
    heads = oq.shape[0]

    def put(i, src, dst, h):
        copy = pltpu.make_async_copy(src.at[h], dst.at[:, pl.ds(h * DH, DH)], sem.at[i, h])
        copy.start()
        return copy

    copies = [put(0, oq, dq, h) for h in range(heads)] + [put(1, og, dg, h) for h in range(heads)]
    for h in range(heads):
        ok[h] = ((glk[h] + mm(v[h], s2[h], NT)) * sk[h]).astype(BF16)
        copies.append(put(2, ok, dk, h))
        ov[h] = (gv[h] + mm(lk[h], s2[h], NN)).astype(BF16)
        copies.append(put(3, ov, dv, h))
    for copy in copies:
        copy.wait()


def per_device(nx, nz, nh, *args):
    rows, width = args[0].shape
    heads = width // DH
    hh = heads // 2
    chips = nx * nz
    piece = hh * DH // chips

    def vmem(dtype, *shape):
        return pltpu.VMEM(shape, dtype)

    low = vmem(BF16, heads, rows, DH)
    wide = vmem(F32, heads, rows, DH)
    low2 = vmem(BF16, hh, rows, DH)
    four = vmem(F32, 4, hh, rows, DH)
    half = vmem(F32, hh, DH, DH)
    pieces = vmem(F32, 2, chips, piece, DH)
    def shape(dtype, *dims):
        return jax.ShapeDtypeStruct(dims, dtype)

    out, out_wide = shape(BF16, heads, rows, DH), shape(F32, heads, rows, DH)
    outs = pl.pallas_call(
        functools.partial(kernel, nx, nz, nh),
        out_shape=(out, out, out, out, out_wide, out_wide, out_wide, shape(BF16, heads, DH, DH)),
        in_specs=[pl.BlockSpec(memory_space=pltpu.HBM)] * 5,
        out_specs=[pl.BlockSpec(memory_space=pltpu.VMEM)] * 8,
        scratch_shapes=[
            low, low, low, low,
            low, wide, wide,
            four, four, low2, low2, low2,
            vmem(F32, 2, hh, rows, DH), vmem(BF16, 2, hh, rows, rows), vmem(BF16, 2, hh, rows, DH),
            vmem(BF16, 2, hh, DH, DH), vmem(BF16, 2, hh, DH, rows),
            vmem(F32, heads, DH, DH), half, vmem(F32, 2, hh, DH, DH), half, half, half,
            pieces, pieces, pieces, pieces, vmem(F32, chips, piece, DH),
            four, four,
            vmem(F32, 2, 1, 2 * rows), vmem(F32, 2 * nh, 2, 1, 2 * rows),
            pltpu.SemaphoreType.DMA((5, heads)), pltpu.SemaphoreType.DMA((11,)), pltpu.SemaphoreType.DMA((11,)),
        ],
        compiler_params=pltpu.CompilerParams(collective_id=0, has_side_effects=True, vmem_limit_bytes=32 << 20),
        name="linear_attention",
    )(*(pltpu.with_memory_space_constraint(a, pltpu.HBM) for a in args))
    return pl.pallas_call(
        finish,
        out_shape=(shape(BF16, rows, width),) * 4,
        in_specs=[pl.BlockSpec(memory_space=pltpu.VMEM)] * 8,
        out_specs=[pl.BlockSpec(memory_space=pltpu.HBM)] * 4,
        scratch_shapes=[low, low, pltpu.SemaphoreType.DMA((4, heads))],
        compiler_params=pltpu.CompilerParams(vmem_limit_bytes=8 << 20),
        name="finish",
    )(*outs)


def solution(mesh):
    nh = mesh.shape["head"]
    nz = NZ
    nx = mesh.shape["ctx"] // (2 * nz)
    spec = P("ctx", "head")
    return jax.shard_map(
        functools.partial(per_device, nx, nz, nh),
        mesh=mesh, in_specs=(spec,) * 5, out_specs=(spec,) * 4, check_vma=False,
    )
```

```python
import functools

import jax
import jax.numpy as jnp
from jax import lax
from jax.experimental import pallas as pl
from jax.experimental.pallas import tpu as pltpu
from jax.sharding import PartitionSpec as P

H = 32
DH = 128
EPSILON = 1e-06
NZ = 8
F32 = jnp.float32
BF16 = jnp.bfloat16

NN = (((1,), (0,)), ((), ()))
NT = (((1,), (1,)), ((), ()))
TN = (((0,), (0,)), ((), ()))


def mm(a, b, dims):
    return lax.dot_general(a, b, dims, preferred_element_type=F32)


def silu_slope(x):
    sig = jax.nn.sigmoid(x)
    return sig * (1.0 + x * (1.0 - sig))


def wrap(value, n):
    return jnp.where(value >= n, value - n, value)


def offsets(nx, nz):
    def away(d, n):
        return min(d, n - d)

    every = [(dx, dz) for dz in range(nz) for dx in range(nx) if dx or dz]
    return sorted(every, key=lambda o: (-away(o[0], nx) - away(o[1], nz), -away(o[1], nz)))


QUICK = 2


def kernel(
    nx, nz, nh,
    q_hbm, k_hbm, v_hbm, g_hbm, c_hbm,
    oq, og, v_ref, lk_ref, glk, gv, sk, s2,
    q_ref, k_ref, g_ref, c_ref,
    lq_ref, gat, gg,
    xo, xi, pq, pk, pv,
    att, wt, da, s1, lqt,
    loc, x_in, loc2, f_out, f_in,
    comb, a_in, p_out, e_in, e_far,
    ro, ri,
    y_out, y_in,
    in_sem, send_sem, recv_sem,
):
    heads, rows, _ = q_ref.shape
    hh = heads // 2
    chips = nx * nz
    piece = hh * DH // chips
    me = lax.axis_index("ctx")
    hd = lax.axis_index("head")
    core = lax.rem(me, 2)
    chip = lax.div(me, 2)
    cx = lax.div(chip, nz)
    cz = lax.rem(chip, nz)
    partner = me + 1 - 2 * core
    quick_chips = [x * nz for x in range(min(QUICK, nx))]
    quick = jnp.logical_and(cz == 0, cx < QUICK)
    give = jnp.logical_not(jnp.logical_and(quick, core == 0))
    take = jnp.logical_not(jnp.logical_and(quick, core == 1))
    own = core * hh
    other = hh - own

    def load(i, src, dst):
        copies = [
            pltpu.make_async_copy(src.at[:, pl.ds(h * DH, DH)], dst.at[h], in_sem.at[i, h])
            for h in range(heads)
        ]
        for copy in copies:
            copy.start()
        return copies

    def arrived(copies):
        for copy in copies:
            copy.wait()

    xs = [wrap(cx + d, nx) * nz for d in range(nx)]
    zs = [wrap(cz + d, nz) for d in range(nz)]
    targets = [xs[dx] + zs[dz] for dx, dz in offsets(nx, nz)]
    far_heads = sorted(range(1, nh), key=lambda d: -min(d, nh - d))
    head_targets = [wrap(hd + d, nh) for d in far_heads]

    barrier = pltpu.get_barrier_semaphore()

    def greet(device):
        pl.semaphore_signal(barrier, inc=1, device_id=device)

    @pl.when(core == 0)
    def _():
        greet({"ctx": partner})

    for to in targets[:6]:
        greet({"ctx": to * 2})
    k_in, v_in = load(0, k_hbm, k_ref), load(1, v_hbm, v_ref)
    for to in targets[6:]:
        greet({"ctx": to * 2})
    for to in head_targets:
        greet({"ctx": chip * 2, "head": to})
    q_in, g_in, c_in = load(2, q_hbm, q_ref), load(3, g_hbm, g_ref), load(4, c_hbm, c_ref)

    def remote(src, dst, stage, device):
        return pltpu.make_async_remote_copy(
            src_ref=src,
            dst_ref=dst,
            send_sem=send_sem.at[stage],
            recv_sem=recv_sem.at[stage],
            device_id=device,
        )

    def scatter(src, dst, stage):
        for to in targets:
            remote(src.at[to], dst.at[chip], stage, {"ctx": to * 2 + core}).start()
        dst[chip] = src[chip]
        n = pl.ds(0, chips - 1)
        return remote(src.at[n], dst.at[n], stage, {"ctx": partner})

    def to_partner(src, dst, stage):
        copy = remote(src, dst, stage, {"ctx": partner})
        copy.start()
        return copy

    def scan_out(scan, total):
        comb[scan] = total.reshape(chips, piece, DH)
        return scatter(comb.at[scan], a_in.at[scan], 2 * scan)

    def scan_back(scan, first, reverse):
        first.wait_recv()
        total = jnp.zeros((piece, DH), F32)
        for i in range(chips):
            j = chips - 1 - i if reverse else i
            p_out[scan, j] = total
            total = total + a_in[scan, j]
        if reverse:

            @pl.when(core == 0)
            def _():
                for to in quick_chips:
                    remote(p_out.at[scan, to], e_far.at[chip], 9, {"ctx": to * 2 + 1}).start()

        return scatter(p_out.at[scan], e_in.at[scan], 2 * scan + 1)

    arrived(k_in)
    arrived(v_in)

    def local(h):
        lk = jax.nn.silu(k_ref[h].astype(F32)).astype(BF16)
        lk_ref[h] = lk
        loc[h] = mm(lk, v_ref[h], TN)

    pair = remote(loc.at[pl.ds(other, hh)], x_in, 4, {"ctx": partner})
    for i in range(hh):
        local(other + i)

    @pl.when(core == 1)
    def _():
        pl.semaphore_wait(barrier, 1)

    @pl.when(core == 0)
    def _():
        pair.wait_recv()

    pair.start()
    for i in range(hh):
        local(own + i)

    @pl.when(core == 1)
    def _():
        pair.wait_recv()

    @pl.when(core == 0)
    def _():
        pl.semaphore_wait(barrier, 2 * (chips - 1) + 2 * (nh - 1))
        greet({"ctx": partner})

    @pl.when(core == 1)
    def _():
        pl.semaphore_wait(barrier, 1)

    first1 = scan_out(0, loc[pl.ds(own, hh)] + x_in[...])

    arrived(q_in)
    arrived(g_in)
    arrived(c_in)

    def lift(h):
        lq_ref[h] = jax.nn.silu(q_ref[h].astype(F32)).astype(BF16)
        sig = jax.nn.sigmoid(g_ref[h].astype(F32))
        gated = c_ref[h].astype(F32) * sig
        gat[h] = gated
        gg[h] = gated * (1.0 - sig)

    for i in range(hh):
        h = other + i
        lift(h)
        xo[0, i] = lq_ref[h].astype(F32)
        xo[1, i] = lk_ref[h].astype(F32)
        xo[2, i] = v_ref[h].astype(F32)
        xo[3, i] = gat[h]
    swap = to_partner(xo, xi, 5)
    row = lax.broadcasted_iota(jnp.int32, (rows, rows), 0)
    col = lax.broadcasted_iota(jnp.int32, (rows, rows), 1)

    def inner(side, i, lq, lk, v):
        w = jnp.where(row >= col, mm(lq, lk, NT), 0.0).astype(BF16)
        att[side, i] = mm(w, v, NN)
        wt[side, i] = jnp.where(col >= row, mm(lk, lq, NT), 0.0).astype(BF16)
        lqt[side, i] = jnp.transpose(lq)

    for i in range(hh):
        lift(own + i)
        inner(0, i, lq_ref[own + i], lk_ref[own + i], v_ref[own + i])
    second1 = scan_back(0, first1, False)
    swap.wait_recv()
    for i in range(hh):
        pq[i] = xi[0, i].astype(BF16)
        pk[i] = xi[1, i].astype(BF16)
        pv[i] = xi[2, i].astype(BF16)
        inner(1, i, pq[i], pk[i], pv[i])

    def operands(side, i):
        if side == 0:
            return lq_ref[own + i], lk_ref[own + i], v_ref[own + i]
        return pq[i], pk[i], pv[i]

    second1.wait_recv()
    state = e_in[0].reshape(hh, DH, DH)
    s1[0] = (state + jnp.where(core == 1, x_in[...], 0.0)).astype(BF16)
    s1[1] = (state + jnp.where(core == 0, loc[pl.ds(own, hh)], 0.0)).astype(BF16)
    parts = []
    for side in range(2):
        sq = jnp.zeros((rows, DH), F32)
        dt = jnp.zeros((rows, DH), F32)
        for i in range(hh):
            a = att[side, i] + mm(operands(side, i)[0], s1[side, i], NN)
            att[side, i] = a
            sq = sq + a * a
            dt = dt + (gat[own + i] if side == 0 else xi[3, i]) * a
        parts += [sq, dt]
    lane = lax.broadcasted_iota(jnp.int32, (rows, DH), 1)
    spread = jnp.zeros((rows, DH), F32)
    for at, part in enumerate(parts):
        spread = jnp.where(lane == at, jnp.sum(part, axis=1, keepdims=True), spread)
    sums = jnp.transpose(spread)
    y_out[core] = jnp.concatenate([sums[0:1], sums[1:2]], axis=1)
    y_out[1 - core] = jnp.concatenate([sums[2:3], sums[3:4]], axis=1)
    slot = hd * 2 + core
    for to in head_targets:
        remote(y_out, y_in.at[slot], 6, {"head": to}).start()
        remote(y_out, y_in.at[slot], 6, {"ctx": partner, "head": to}).start()
    remote(y_out, y_in.at[slot], 6, {"ctx": partner}).start()
    y_in[slot] = y_out[...]
    n = pl.ds(0, 2 * nh - 1)
    y_all = remote(y_in.at[n], y_in.at[n], 6, {"ctx": partner})
    y_all.wait_recv()
    full = nh * heads * DH
    lanes = []
    for side in range(2):
        block = core if side == 0 else 1 - core
        tot = y_in[0, block]
        for j in range(1, 2 * nh):
            tot = tot + y_in[j, block]
        rinv = lax.rsqrt(tot[:, 0:rows] / full + EPSILON)
        lanes += [rinv, (tot[:, rows : 2 * rows] * rinv / full) * rinv * rinv]
    sub = lax.broadcasted_iota(jnp.int32, (8, lanes[0].shape[1]), 0)
    stacked = jnp.where(sub == 0, lanes[0], jnp.where(sub == 1, lanes[1], jnp.where(sub == 2, lanes[2], lanes[3])))
    columns = jnp.transpose(stacked)
    rinv_c = [columns[:, 0:1], columns[:, 2:3]]
    coef_c = [columns[:, 1:2], columns[:, 3:4]]
    for side in range(2):
        for i in range(hh):
            gated = gat[own + i] if side == 0 else xi[3, i]
            d = (gated * rinv_c[side] - att[side, i] * coef_c[side]).astype(BF16)
            da[side, i] = d
            loc2[side, i] = mm(lqt[side, i], d, NN)
    first2 = scan_out(1, loc2[0] + loc2[1])

    def inside(side, i):
        lq, lk, v = operands(side, i)
        d = da[side, i]
        dw = jnp.where(row >= col, mm(d, v, NT), 0.0).astype(BF16)
        dwt = jnp.where(col >= row, mm(v, d, NT), 0.0).astype(BF16)
        glq = mm(dw, lk, NN) + mm(d, s1[side, i], NT)
        return att[side, i] * rinv_c[side], glq, mm(dwt, lq, NN), mm(wt[side, i], d, NN)

    for i in range(hh):
        ro[0, i], ro[1, i], ro[2, i], ro[3, i] = inside(1, i)
    back = to_partner(ro, ri, 7)
    second2 = scan_back(1, first2, True)

    def settle(h, normed, glq):
        og[h] = (gg[h] * normed).astype(BF16)
        oq[h] = (glq * silu_slope(q_ref[h].astype(F32))).astype(BF16)
        sk[h] = silu_slope(k_ref[h].astype(F32))

    for i in range(hh):
        normed, glq, glk[own + i], gv[own + i] = inside(0, i)
        settle(own + i, normed, glq)
    back.wait_recv()
    for i in range(hh):
        settle(other + i, ri[0, i], ri[1, i])
        glk[other + i] = ri[2, i]
        gv[other + i] = ri[3, i]

    second2.wait_recv()
    state = e_in[1].reshape(hh, DH, DH)
    s2[pl.ds(own, hh)] = (state + jnp.where(core == 0, loc2[1], 0.0)).astype(BF16)

    last = remote(f_out, f_in, 8, {"ctx": partner})

    @pl.when(give)
    def _():
        f_out[...] = state + jnp.where(core == 1, loc2[0], 0.0)
        last.start()

    @pl.when(take)
    def _():
        last.wait_recv()
        s2[pl.ds(other, hh)] = f_in[...].astype(BF16)

    @pl.when(jnp.logical_not(take))
    def _():
        remote(e_far, e_far, 9, {"ctx": partner}).wait_recv()
        s2[pl.ds(other, hh)] = e_far[...].reshape(hh, DH, DH).astype(BF16)

    @pl.when(give)
    def _():
        last.wait_send()

    @pl.when(core == 0)
    def _():
        n = pl.ds(0, len(quick_chips))
        remote(p_out.at[1, n], e_far.at[n], 9, {"ctx": partner}).wait_send()

    for sent in (pair, first1, swap, second1, y_all, first2, back, second2):
        sent.wait_send()


def finish(oq, og, v, lk, glk, gv, sk, s2, dq, dk, dv, dg, ok, ov, sem):
    heads = oq.shape[0]

    def put(i, src, dst, h):
        copy = pltpu.make_async_copy(src.at[h], dst.at[:, pl.ds(h * DH, DH)], sem.at[i, h])
        copy.start()
        return copy

    copies = [put(0, oq, dq, h) for h in range(heads)] + [put(1, og, dg, h) for h in range(heads)]
    for h in range(heads):
        ok[h] = ((glk[h] + mm(v[h], s2[h], NT)) * sk[h]).astype(BF16)
        copies.append(put(2, ok, dk, h))
        ov[h] = (gv[h] + mm(lk[h], s2[h], NN)).astype(BF16)
        copies.append(put(3, ov, dv, h))
    for copy in copies:
        copy.wait()


def per_device(nx, nz, nh, *args):
    rows, width = args[0].shape
    heads = width // DH
    hh = heads // 2
    chips = nx * nz
    piece = hh * DH // chips

    def vmem(dtype, *shape):
        return pltpu.VMEM(shape, dtype)

    low = vmem(BF16, heads, rows, DH)
    wide = vmem(F32, heads, rows, DH)
    low2 = vmem(BF16, hh, rows, DH)
    four = vmem(F32, 4, hh, rows, DH)
    half = vmem(F32, hh, DH, DH)
    pieces = vmem(F32, 2, chips, piece, DH)
    def shape(dtype, *dims):
        return jax.ShapeDtypeStruct(dims, dtype)

    out, out_wide = shape(BF16, heads, rows, DH), shape(F32, heads, rows, DH)
    outs = pl.pallas_call(
        functools.partial(kernel, nx, nz, nh),
        out_shape=(out, out, out, out, out_wide, out_wide, out_wide, shape(BF16, heads, DH, DH)),
        in_specs=[pl.BlockSpec(memory_space=pltpu.HBM)] * 5,
        out_specs=[pl.BlockSpec(memory_space=pltpu.VMEM)] * 8,
        scratch_shapes=[
            low, low, low, low,
            low, wide, wide,
            four, four, low2, low2, low2,
            vmem(F32, 2, hh, rows, DH), vmem(BF16, 2, hh, rows, rows), vmem(BF16, 2, hh, rows, DH),
            vmem(BF16, 2, hh, DH, DH), vmem(BF16, 2, hh, DH, rows),
            vmem(F32, heads, DH, DH), half, vmem(F32, 2, hh, DH, DH), half, half,
            pieces, pieces, pieces, pieces, vmem(F32, chips, piece, DH),
            four, four,
            vmem(F32, 2, 1, 2 * rows), vmem(F32, 2 * nh, 2, 1, 2 * rows),
            pltpu.SemaphoreType.DMA((5, heads)), pltpu.SemaphoreType.DMA((10,)), pltpu.SemaphoreType.DMA((10,)),
        ],
        compiler_params=pltpu.CompilerParams(collective_id=0, has_side_effects=True, vmem_limit_bytes=32 << 20),
        name="linear_attention",
    )(*(pltpu.with_memory_space_constraint(a, pltpu.HBM) for a in args))
    return pl.pallas_call(
        finish,
        out_shape=(shape(BF16, rows, width),) * 4,
        in_specs=[pl.BlockSpec(memory_space=pltpu.VMEM)] * 8,
        out_specs=[pl.BlockSpec(memory_space=pltpu.HBM)] * 4,
        scratch_shapes=[low, low, pltpu.SemaphoreType.DMA((4, heads))],
        compiler_params=pltpu.CompilerParams(vmem_limit_bytes=8 << 20),
        name="finish",
    )(*outs)


def solution(mesh):
    nh = mesh.shape["head"]
    nz = NZ
    nx = mesh.shape["ctx"] // (2 * nz)
    spec = P("ctx", "head")
    return jax.shard_map(
        functools.partial(per_device, nx, nz, nh),
        mesh=mesh, in_specs=(spec,) * 5, out_specs=(spec,) * 4, check_vma=False,
    )
```

```python
import functools

import jax
import jax.numpy as jnp
from jax import lax
from jax.experimental import pallas as pl
from jax.experimental.pallas import tpu as pltpu
from jax.sharding import PartitionSpec as P

H = 32
DH = 128
EPSILON = 1e-06
NZ = 8
F32 = jnp.float32
BF16 = jnp.bfloat16

NN = (((1,), (0,)), ((), ()))
NT = (((1,), (1,)), ((), ()))
TN = (((0,), (0,)), ((), ()))


def mm(a, b, dims):
    return lax.dot_general(a, b, dims, preferred_element_type=F32)


def silu_slope(x):
    sig = jax.nn.sigmoid(x)
    return sig * (1.0 + x * (1.0 - sig))


def wrap(value, n):
    return jnp.where(value >= n, value - n, value)


def offsets(nx, nz):
    def away(d, n):
        return min(d, n - d)

    every = [(dx, dz) for dz in range(nz) for dx in range(nx) if dx or dz]
    return sorted(every, key=lambda o: (-away(o[0], nx) - away(o[1], nz), -away(o[1], nz)))


QUICK = 2


def kernel(
    nx, nz, nh,
    q_hbm, k_hbm, v_hbm, g_hbm, c_hbm,
    oq, og, v_ref, lk_ref, glk, gv, sk, s2,
    q_ref, k_ref, g_ref, c_ref,
    lq_ref, gat, gg,
    xo, xi, pq, pk, pv,
    att, wt, da, s1, lqt,
    loc, x_in, loc2, f_out, f_in,
    comb, a_in, p_out, e_in, e_far,
    ro, ri,
    y_out, y_in,
    in_sem, send_sem, recv_sem,
):
    heads, rows, _ = q_ref.shape
    hh = heads // 2
    chips = nx * nz
    piece = hh * DH // chips
    me = lax.axis_index("ctx")
    hd = lax.axis_index("head")
    core = lax.rem(me, 2)
    chip = lax.div(me, 2)
    cx = lax.div(chip, nz)
    cz = lax.rem(chip, nz)
    partner = me + 1 - 2 * core
    quick_chips = [x * nz for x in range(min(QUICK, nx))]
    quick = jnp.logical_and(cz == 0, cx < QUICK)
    give = jnp.logical_not(jnp.logical_and(quick, core == 0))
    take = jnp.logical_not(jnp.logical_and(quick, core == 1))
    own = core * hh
    other = hh - own

    def load(i, src, dst):
        copies = [
            pltpu.make_async_copy(src.at[:, pl.ds(h * DH, DH)], dst.at[h], in_sem.at[i, h])
            for h in range(heads)
        ]
        for copy in copies:
            copy.start()
        return copies

    def arrived(copies):
        for copy in copies:
            copy.wait()

    xs = [wrap(cx + d, nx) * nz for d in range(nx)]
    zs = [wrap(cz + d, nz) for d in range(nz)]
    targets = [xs[dx] + zs[dz] for dx, dz in offsets(nx, nz)]
    far_heads = sorted(range(1, nh), key=lambda d: -min(d, nh - d))
    head_targets = [wrap(hd + d, nh) for d in far_heads]

    barrier = pltpu.get_barrier_semaphore()

    def greet(device):
        pl.semaphore_signal(barrier, inc=1, device_id=device)

    @pl.when(core == 0)
    def _():
        greet({"ctx": partner})

    for to in targets[:6]:
        greet({"ctx": to * 2})
    k_in, v_in = load(0, k_hbm, k_ref), load(1, v_hbm, v_ref)
    for to in targets[6:]:
        greet({"ctx": to * 2})
    for to in head_targets:
        greet({"ctx": chip * 2, "head": to})
    q_in, g_in, c_in = load(2, q_hbm, q_ref), load(3, g_hbm, g_ref), load(4, c_hbm, c_ref)

    def remote(src, dst, stage, device):
        return pltpu.make_async_remote_copy(
            src_ref=src,
            dst_ref=dst,
            send_sem=send_sem.at[stage],
            recv_sem=recv_sem.at[stage],
            device_id=device,
        )

    def scatter(src, dst, stage):
        for to in targets:
            remote(src.at[to], dst.at[chip], stage, {"ctx": to * 2 + core}).start()
        dst[chip] = src[chip]
        n = pl.ds(0, chips - 1)
        return remote(src.at[n], dst.at[n], stage, {"ctx": partner})

    def to_partner(src, dst, stage):
        copy = remote(src, dst, stage, {"ctx": partner})
        copy.start()
        return copy

    def scan_out(scan, total):
        comb[scan] = total.reshape(chips, piece, DH)
        return scatter(comb.at[scan], a_in.at[scan], 2 * scan)

    def scan_back(scan, first, reverse):
        first.wait_recv()
        total = jnp.zeros((piece, DH), F32)
        for i in range(chips):
            j = chips - 1 - i if reverse else i
            p_out[scan, j] = total
            total = total + a_in[scan, j]
        if reverse:

            @pl.when(core == 0)
            def _():
                for to in quick_chips:
                    remote(p_out.at[scan, to], e_far.at[chip], 9, {"ctx": to * 2 + 1}).start()

        return scatter(p_out.at[scan], e_in.at[scan], 2 * scan + 1)

    arrived(k_in)
    arrived(v_in)

    def local(h):
        lk = jax.nn.silu(k_ref[h].astype(F32)).astype(BF16)
        lk_ref[h] = lk
        loc[h] = mm(lk, v_ref[h], TN)

    pair = remote(loc.at[pl.ds(other, hh)], x_in, 4, {"ctx": partner})
    for i in range(hh):
        local(other + i)

    @pl.when(core == 1)
    def _():
        pl.semaphore_wait(barrier, 1)

    @pl.when(core == 0)
    def _():
        pair.wait_recv()

    pair.start()
    for i in range(hh):
        local(own + i)

    @pl.when(core == 1)
    def _():
        pair.wait_recv()

    @pl.when(core == 0)
    def _():
        pl.semaphore_wait(barrier, 2 * (chips - 1) + 2 * (nh - 1))
        greet({"ctx": partner})

    @pl.when(core == 1)
    def _():
        pl.semaphore_wait(barrier, 1)

    first1 = scan_out(0, loc[pl.ds(own, hh)] + x_in[...])

    arrived(q_in)
    arrived(g_in)
    arrived(c_in)

    def lift(h):
        lq_ref[h] = jax.nn.silu(q_ref[h].astype(F32)).astype(BF16)
        sig = jax.nn.sigmoid(g_ref[h].astype(F32))
        gated = c_ref[h].astype(F32) * sig
        gat[h] = gated
        gg[h] = gated * (1.0 - sig)

    for i in range(hh):
        h = other + i
        lift(h)
        xo[0, i] = lq_ref[h].astype(F32)
        xo[1, i] = lk_ref[h].astype(F32)
        xo[2, i] = v_ref[h].astype(F32)
        xo[3, i] = gat[h]
    swap = to_partner(xo, xi, 5)
    row = lax.broadcasted_iota(jnp.int32, (rows, rows), 0)
    col = lax.broadcasted_iota(jnp.int32, (rows, rows), 1)

    def inner(side, i, lq, lk, v):
        w = jnp.where(row >= col, mm(lq, lk, NT), 0.0).astype(BF16)
        att[side, i] = mm(w, v, NN)
        wt[side, i] = jnp.where(col >= row, mm(lk, lq, NT), 0.0).astype(BF16)
        lqt[i, :, side * rows : (side + 1) * rows] = jnp.transpose(lq)

    for i in range(hh):
        lift(own + i)
        inner(0, i, lq_ref[own + i], lk_ref[own + i], v_ref[own + i])
    second1 = scan_back(0, first1, False)
    swap.wait_recv()
    for i in range(hh):
        pq[i] = xi[0, i].astype(BF16)
        pk[i] = xi[1, i].astype(BF16)
        pv[i] = xi[2, i].astype(BF16)
        inner(1, i, pq[i], pk[i], pv[i])

    def operands(side, i):
        if side == 0:
            return lq_ref[own + i], lk_ref[own + i], v_ref[own + i]
        return pq[i], pk[i], pv[i]

    second1.wait_recv()
    state = e_in[0].reshape(hh, DH, DH)
    s1[0] = (state + jnp.where(core == 1, x_in[...], 0.0)).astype(BF16)
    s1[1] = (state + jnp.where(core == 0, loc[pl.ds(own, hh)], 0.0)).astype(BF16)
    parts = []
    for side in range(2):
        sq = jnp.zeros((rows, DH), F32)
        dt = jnp.zeros((rows, DH), F32)
        for i in range(hh):
            a = att[side, i] + mm(operands(side, i)[0], s1[side, i], NN)
            att[side, i] = a
            sq = sq + a * a
            dt = dt + (gat[own + i] if side == 0 else xi[3, i]) * a
        parts += [sq, dt]
    lane = lax.broadcasted_iota(jnp.int32, (rows, DH), 1)
    spread = jnp.zeros((rows, DH), F32)
    for at, part in enumerate(parts):
        spread = jnp.where(lane == at, jnp.sum(part, axis=1, keepdims=True), spread)
    sums = jnp.transpose(spread)
    y_out[core] = jnp.concatenate([sums[0:1], sums[1:2]], axis=1)
    y_out[1 - core] = jnp.concatenate([sums[2:3], sums[3:4]], axis=1)
    slot = hd * 2 + core
    for to in head_targets:
        remote(y_out, y_in.at[slot], 6, {"head": to}).start()
        remote(y_out, y_in.at[slot], 6, {"ctx": partner, "head": to}).start()
    remote(y_out, y_in.at[slot], 6, {"ctx": partner}).start()
    y_in[slot] = y_out[...]
    n = pl.ds(0, 2 * nh - 1)
    y_all = remote(y_in.at[n], y_in.at[n], 6, {"ctx": partner})
    y_all.wait_recv()
    full = nh * heads * DH
    lanes = []
    for side in range(2):
        block = core if side == 0 else 1 - core
        tot = y_in[0, block]
        for j in range(1, 2 * nh):
            tot = tot + y_in[j, block]
        rinv = lax.rsqrt(tot[:, 0:rows] / full + EPSILON)
        lanes += [rinv, (tot[:, rows : 2 * rows] * rinv / full) * rinv * rinv]
    sub = lax.broadcasted_iota(jnp.int32, (8, lanes[0].shape[1]), 0)
    stacked = jnp.where(sub == 0, lanes[0], jnp.where(sub == 1, lanes[1], jnp.where(sub == 2, lanes[2], lanes[3])))
    columns = jnp.transpose(stacked)
    rinv_c = [columns[:, 0:1], columns[:, 2:3]]
    coef_c = [columns[:, 1:2], columns[:, 3:4]]
    for side in range(2):
        for i in range(hh):
            gated = gat[own + i] if side == 0 else xi[3, i]
            d = (gated * rinv_c[side] - att[side, i] * coef_c[side]).astype(BF16)
            da[i, side * rows : (side + 1) * rows] = d
    first2 = scan_out(1, jnp.stack([mm(lqt[i], da[i], NN) for i in range(hh)]))
    for i in range(hh):
        loc2[0, i] = mm(lqt[i, :, 0:rows], da[i, 0:rows], NN)
        loc2[1, i] = mm(lqt[i, :, rows : 2 * rows], da[i, rows : 2 * rows], NN)

    def inside(side, i):
        lq, lk, v = operands(side, i)
        d = da[i, side * rows : (side + 1) * rows]
        dw = jnp.where(row >= col, mm(d, v, NT), 0.0).astype(BF16)
        dwt = jnp.where(col >= row, mm(v, d, NT), 0.0).astype(BF16)
        glq = mm(dw, lk, NN) + mm(d, s1[side, i], NT)
        return att[side, i] * rinv_c[side], glq, mm(dwt, lq, NN), mm(wt[side, i], d, NN)

    for i in range(hh):
        ro[0, i], ro[1, i], ro[2, i], ro[3, i] = inside(1, i)
    back = to_partner(ro, ri, 7)
    second2 = scan_back(1, first2, True)

    def settle(h, normed, glq):
        og[h] = (gg[h] * normed).astype(BF16)
        oq[h] = (glq * silu_slope(q_ref[h].astype(F32))).astype(BF16)
        sk[h] = silu_slope(k_ref[h].astype(F32))

    for i in range(hh):
        normed, glq, glk[own + i], gv[own + i] = inside(0, i)
        settle(own + i, normed, glq)
    back.wait_recv()
    for i in range(hh):
        settle(other + i, ri[0, i], ri[1, i])
        glk[other + i] = ri[2, i]
        gv[other + i] = ri[3, i]

    second2.wait_recv()
    state = e_in[1].reshape(hh, DH, DH)
    s2[pl.ds(own, hh)] = (state + jnp.where(core == 0, loc2[1], 0.0)).astype(BF16)

    last = remote(f_out, f_in, 8, {"ctx": partner})

    @pl.when(give)
    def _():
        f_out[...] = state + jnp.where(core == 1, loc2[0], 0.0)
        last.start()

    @pl.when(take)
    def _():
        last.wait_recv()
        s2[pl.ds(other, hh)] = f_in[...].astype(BF16)

    @pl.when(jnp.logical_not(take))
    def _():
        remote(e_far, e_far, 9, {"ctx": partner}).wait_recv()
        s2[pl.ds(other, hh)] = e_far[...].reshape(hh, DH, DH).astype(BF16)

    @pl.when(give)
    def _():
        last.wait_send()

    @pl.when(core == 0)
    def _():
        n = pl.ds(0, len(quick_chips))
        remote(p_out.at[1, n], e_far.at[n], 9, {"ctx": partner}).wait_send()

    for sent in (pair, first1, swap, second1, y_all, first2, back, second2):
        sent.wait_send()


def finish(oq, og, v, lk, glk, gv, sk, s2, dq, dk, dv, dg, ok, ov, sem):
    heads = oq.shape[0]

    def put(i, src, dst, h):
        copy = pltpu.make_async_copy(src.at[h], dst.at[:, pl.ds(h * DH, DH)], sem.at[i, h])
        copy.start()
        return copy

    copies = [put(0, oq, dq, h) for h in range(heads)] + [put(1, og, dg, h) for h in range(heads)]
    for h in range(heads):
        ok[h] = ((glk[h] + mm(v[h], s2[h], NT)) * sk[h]).astype(BF16)
        copies.append(put(2, ok, dk, h))
        ov[h] = (gv[h] + mm(lk[h], s2[h], NN)).astype(BF16)
        copies.append(put(3, ov, dv, h))
    for copy in copies:
        copy.wait()


def per_device(nx, nz, nh, *args):
    rows, width = args[0].shape
    heads = width // DH
    hh = heads // 2
    chips = nx * nz
    piece = hh * DH // chips

    def vmem(dtype, *shape):
        return pltpu.VMEM(shape, dtype)

    low = vmem(BF16, heads, rows, DH)
    wide = vmem(F32, heads, rows, DH)
    low2 = vmem(BF16, hh, rows, DH)
    four = vmem(F32, 4, hh, rows, DH)
    half = vmem(F32, hh, DH, DH)
    pieces = vmem(F32, 2, chips, piece, DH)
    def shape(dtype, *dims):
        return jax.ShapeDtypeStruct(dims, dtype)

    out, out_wide = shape(BF16, heads, rows, DH), shape(F32, heads, rows, DH)
    outs = pl.pallas_call(
        functools.partial(kernel, nx, nz, nh),
        out_shape=(out, out, out, out, out_wide, out_wide, out_wide, shape(BF16, heads, DH, DH)),
        in_specs=[pl.BlockSpec(memory_space=pltpu.HBM)] * 5,
        out_specs=[pl.BlockSpec(memory_space=pltpu.VMEM)] * 8,
        scratch_shapes=[
            low, low, low, low,
            low, wide, wide,
            four, four, low2, low2, low2,
            vmem(F32, 2, hh, rows, DH), vmem(BF16, 2, hh, rows, rows), vmem(BF16, hh, 2 * rows, DH),
            vmem(BF16, 2, hh, DH, DH), vmem(BF16, hh, DH, 2 * rows),
            vmem(F32, heads, DH, DH), half, vmem(F32, 2, hh, DH, DH), half, half,
            pieces, pieces, pieces, pieces, vmem(F32, chips, piece, DH),
            four, four,
            vmem(F32, 2, 1, 2 * rows), vmem(F32, 2 * nh, 2, 1, 2 * rows),
            pltpu.SemaphoreType.DMA((5, heads)), pltpu.SemaphoreType.DMA((10,)), pltpu.SemaphoreType.DMA((10,)),
        ],
        compiler_params=pltpu.CompilerParams(collective_id=0, has_side_effects=True, vmem_limit_bytes=32 << 20),
        name="linear_attention",
    )(*(pltpu.with_memory_space_constraint(a, pltpu.HBM) for a in args))
    return pl.pallas_call(
        finish,
        out_shape=(shape(BF16, rows, width),) * 4,
        in_specs=[pl.BlockSpec(memory_space=pltpu.VMEM)] * 8,
        out_specs=[pl.BlockSpec(memory_space=pltpu.HBM)] * 4,
        scratch_shapes=[low, low, pltpu.SemaphoreType.DMA((4, heads))],
        compiler_params=pltpu.CompilerParams(vmem_limit_bytes=8 << 20),
        name="finish",
    )(*outs)


def solution(mesh):
    nh = mesh.shape["head"]
    nz = NZ
    nx = mesh.shape["ctx"] // (2 * nz)
    spec = P("ctx", "head")
    return jax.shard_map(
        functools.partial(per_device, nx, nz, nh),
        mesh=mesh, in_specs=(spec,) * 5, out_specs=(spec,) * 4, check_vma=False,
    )
```

```python
import functools

import jax
import jax.numpy as jnp
from jax import lax
from jax.experimental import pallas as pl
from jax.experimental.pallas import tpu as pltpu
from jax.sharding import PartitionSpec as P

H = 32
DH = 128
EPSILON = 1e-06
NZ = 8
F32 = jnp.float32
BF16 = jnp.bfloat16

NN = (((1,), (0,)), ((), ()))
NT = (((1,), (1,)), ((), ()))
TN = (((0,), (0,)), ((), ()))


def mm(a, b, dims):
    return lax.dot_general(a, b, dims, preferred_element_type=F32)


def silu_slope(x):
    sig = jax.nn.sigmoid(x)
    return sig * (1.0 + x * (1.0 - sig))


def wrap(value, n):
    return jnp.where(value >= n, value - n, value)


def offsets(nx, nz):
    def away(d, n):
        return min(d, n - d)

    every = [(dx, dz) for dz in range(nz) for dx in range(nx) if dx or dz]
    return sorted(every, key=lambda o: (-away(o[0], nx) - away(o[1], nz), -away(o[1], nz)))


QUICK = 1


def kernel(
    nx, nz, nh,
    q_hbm, k_hbm, v_hbm, g_hbm, c_hbm,
    oq, og, v_ref, lk_ref, glk, gv, sk, s2,
    q_ref, k_ref, g_ref, c_ref,
    lq_ref, gat, gg,
    xo, xi, pq, pk, pv,
    att, wt, da, s1, lqt,
    loc, x_in, loc2, f_out, f_in,
    comb, a_in, p_out, e_in, e_far,
    ro, ri,
    y_out, y_in,
    in_sem, send_sem, recv_sem,
):
    heads, rows, _ = q_ref.shape
    hh = heads // 2
    chips = nx * nz
    piece = hh * DH // chips
    me = lax.axis_index("ctx")
    hd = lax.axis_index("head")
    core = lax.rem(me, 2)
    chip = lax.div(me, 2)
    cx = lax.div(chip, nz)
    cz = lax.rem(chip, nz)
    partner = me + 1 - 2 * core
    quick_chips = [x * nz for x in range(min(QUICK, nx))]
    quick = jnp.logical_and(cz == 0, cx < QUICK)
    give = jnp.logical_not(jnp.logical_and(quick, core == 0))
    take = jnp.logical_not(jnp.logical_and(quick, core == 1))
    own = core * hh
    other = hh - own

    def load(i, src, dst):
        copies = [
            pltpu.make_async_copy(src.at[:, pl.ds(h * DH, DH)], dst.at[h], in_sem.at[i, h])
            for h in range(heads)
        ]
        for copy in copies:
            copy.start()
        return copies

    def arrived(copies):
        for copy in copies:
            copy.wait()

    xs = [wrap(cx + d, nx) * nz for d in range(nx)]
    zs = [wrap(cz + d, nz) for d in range(nz)]
    targets = [xs[dx] + zs[dz] for dx, dz in offsets(nx, nz)]
    far_heads = sorted(range(1, nh), key=lambda d: -min(d, nh - d))
    head_targets = [wrap(hd + d, nh) for d in far_heads]

    barrier = pltpu.get_barrier_semaphore()

    def greet(device):
        pl.semaphore_signal(barrier, inc=1, device_id=device)

    @pl.when(core == 0)
    def _():
        greet({"ctx": partner})

    for to in targets[:6]:
        greet({"ctx": to * 2})
    k_in, v_in = load(0, k_hbm, k_ref), load(1, v_hbm, v_ref)
    for to in targets[6:]:
        greet({"ctx": to * 2})
    for to in head_targets:
        greet({"ctx": chip * 2, "head": to})
    q_in, g_in, c_in = load(2, q_hbm, q_ref), load(3, g_hbm, g_ref), load(4, c_hbm, c_ref)

    def remote(src, dst, stage, device):
        return pltpu.make_async_remote_copy(
            src_ref=src,
            dst_ref=dst,
            send_sem=send_sem.at[stage],
            recv_sem=recv_sem.at[stage],
            device_id=device,
        )

    def scatter(src, dst, stage):
        for to in targets:
            remote(src.at[to], dst.at[chip], stage, {"ctx": to * 2 + core}).start()
        dst[chip] = src[chip]
        n = pl.ds(0, chips - 1)
        return remote(src.at[n], dst.at[n], stage, {"ctx": partner})

    def to_partner(src, dst, stage):
        copy = remote(src, dst, stage, {"ctx": partner})
        copy.start()
        return copy

    def scan_out(scan, total):
        comb[scan] = total.reshape(chips, piece, DH)
        return scatter(comb.at[scan], a_in.at[scan], 2 * scan)

    def scan_back(scan, first, reverse):
        first.wait_recv()
        total = jnp.zeros((piece, DH), F32)
        for i in range(chips):
            j = chips - 1 - i if reverse else i
            p_out[scan, j] = total
            total = total + a_in[scan, j]
        if reverse:

            @pl.when(core == 0)
            def _():
                for to in quick_chips:
                    remote(p_out.at[scan, to], e_far.at[chip], 9, {"ctx": to * 2 + 1}).start()

        return scatter(p_out.at[scan], e_in.at[scan], 2 * scan + 1)

    arrived(k_in)
    arrived(v_in)

    def local(h):
        lk = jax.nn.silu(k_ref[h].astype(F32)).astype(BF16)
        lk_ref[h] = lk
        loc[h] = mm(lk, v_ref[h], TN)

    pair = remote(loc.at[pl.ds(other, hh)], x_in, 4, {"ctx": partner})
    for i in range(hh):
        local(other + i)

    @pl.when(core == 1)
    def _():
        pl.semaphore_wait(barrier, 1)

    @pl.when(core == 0)
    def _():
        pair.wait_recv()

    pair.start()
    for i in range(hh):
        local(own + i)

    @pl.when(core == 1)
    def _():
        pair.wait_recv()

    @pl.when(core == 0)
    def _():
        pl.semaphore_wait(barrier, 2 * (chips - 1) + 2 * (nh - 1))
        greet({"ctx": partner})

    @pl.when(core == 1)
    def _():
        pl.semaphore_wait(barrier, 1)

    first1 = scan_out(0, loc[pl.ds(own, hh)] + x_in[...])

    arrived(q_in)
    arrived(g_in)
    arrived(c_in)

    def lift(h):
        lq_ref[h] = jax.nn.silu(q_ref[h].astype(F32)).astype(BF16)
        sig = jax.nn.sigmoid(g_ref[h].astype(F32))
        gated = c_ref[h].astype(F32) * sig
        gat[h] = gated
        gg[h] = gated * (1.0 - sig)

    for i in range(hh):
        h = other + i
        lift(h)
        xo[0, i] = lq_ref[h].astype(F32)
        xo[1, i] = lk_ref[h].astype(F32)
        xo[2, i] = v_ref[h].astype(F32)
        xo[3, i] = gat[h]
    swap = to_partner(xo, xi, 5)
    row = lax.broadcasted_iota(jnp.int32, (rows, rows), 0)
    col = lax.broadcasted_iota(jnp.int32, (rows, rows), 1)

    def inner(side, i, lq, lk, v):
        w = jnp.where(row >= col, mm(lq, lk, NT), 0.0).astype(BF16)
        att[side, i] = mm(w, v, NN)
        wt[side, i] = jnp.where(col >= row, mm(lk, lq, NT), 0.0).astype(BF16)
        lqt[side, i] = jnp.transpose(lq)

    for i in range(hh):
        lift(own + i)
        inner(0, i, lq_ref[own + i], lk_ref[own + i], v_ref[own + i])
    second1 = scan_back(0, first1, False)
    swap.wait_recv()
    for i in range(hh):
        pq[i] = xi[0, i].astype(BF16)
        pk[i] = xi[1, i].astype(BF16)
        pv[i] = xi[2, i].astype(BF16)
        inner(1, i, pq[i], pk[i], pv[i])

    def operands(side, i):
        if side == 0:
            return lq_ref[own + i], lk_ref[own + i], v_ref[own + i]
        return pq[i], pk[i], pv[i]

    second1.wait_recv()
    state = e_in[0].reshape(hh, DH, DH)
    s1[0] = (state + jnp.where(core == 1, x_in[...], 0.0)).astype(BF16)
    s1[1] = (state + jnp.where(core == 0, loc[pl.ds(own, hh)], 0.0)).astype(BF16)
    parts = []
    for side in range(2):
        sq = jnp.zeros((rows, DH), F32)
        dt = jnp.zeros((rows, DH), F32)
        for i in range(hh):
            a = att[side, i] + mm(operands(side, i)[0], s1[side, i], NN)
            att[side, i] = a
            sq = sq + a * a
            dt = dt + (gat[own + i] if side == 0 else xi[3, i]) * a
        parts += [sq, dt]
    lane = lax.broadcasted_iota(jnp.int32, (rows, DH), 1)
    spread = jnp.zeros((rows, DH), F32)
    for at, part in enumerate(parts):
        spread = jnp.where(lane == at, jnp.sum(part, axis=1, keepdims=True), spread)
    sums = jnp.transpose(spread)
    y_out[core] = jnp.concatenate([sums[0:1], sums[1:2]], axis=1)
    y_out[1 - core] = jnp.concatenate([sums[2:3], sums[3:4]], axis=1)
    slot = hd * 2 + core
    for to in head_targets:
        remote(y_out, y_in.at[slot], 6, {"head": to}).start()
        remote(y_out, y_in.at[slot], 6, {"ctx": partner, "head": to}).start()
    remote(y_out, y_in.at[slot], 6, {"ctx": partner}).start()
    y_in[slot] = y_out[...]
    n = pl.ds(0, 2 * nh - 1)
    y_all = remote(y_in.at[n], y_in.at[n], 6, {"ctx": partner})
    y_all.wait_recv()
    full = nh * heads * DH
    lanes = []
    for side in range(2):
        block = core if side == 0 else 1 - core
        tot = y_in[0, block]
        for j in range(1, 2 * nh):
            tot = tot + y_in[j, block]
        rinv = lax.rsqrt(tot[:, 0:rows] / full + EPSILON)
        lanes += [rinv, (tot[:, rows : 2 * rows] * rinv / full) * rinv * rinv]
    sub = lax.broadcasted_iota(jnp.int32, (8, lanes[0].shape[1]), 0)
    stacked = jnp.where(sub == 0, lanes[0], jnp.where(sub == 1, lanes[1], jnp.where(sub == 2, lanes[2], lanes[3])))
    columns = jnp.transpose(stacked)
    rinv_c = [columns[:, 0:1], columns[:, 2:3]]
    coef_c = [columns[:, 1:2], columns[:, 3:4]]
    for side in range(2):
        for i in range(hh):
            gated = gat[own + i] if side == 0 else xi[3, i]
            d = (gated * rinv_c[side] - att[side, i] * coef_c[side]).astype(BF16)
            da[side, i] = d
            loc2[side, i] = mm(lqt[side, i], d, NN)
    first2 = scan_out(1, loc2[0] + loc2[1])

    def inside(side, i):
        lq, lk, v = operands(side, i)
        d = da[side, i]
        dw = jnp.where(row >= col, mm(d, v, NT), 0.0).astype(BF16)
        dwt = jnp.where(col >= row, mm(v, d, NT), 0.0).astype(BF16)
        glq = mm(dw, lk, NN) + mm(d, s1[side, i], NT)
        return att[side, i] * rinv_c[side], glq, mm(dwt, lq, NN), mm(wt[side, i], d, NN)

    for i in range(hh):
        ro[0, i], ro[1, i], ro[2, i], ro[3, i] = inside(1, i)
    back = to_partner(ro, ri, 7)
    second2 = scan_back(1, first2, True)

    def settle(h, normed, glq):
        og[h] = (gg[h] * normed).astype(BF16)
        oq[h] = (glq * silu_slope(q_ref[h].astype(F32))).astype(BF16)
        sk[h] = silu_slope(k_ref[h].astype(F32))

    for i in range(hh):
        normed, glq, glk[own + i], gv[own + i] = inside(0, i)
        settle(own + i, normed, glq)
    back.wait_recv()
    for i in range(hh):
        settle(other + i, ri[0, i], ri[1, i])
        glk[other + i] = ri[2, i]
        gv[other + i] = ri[3, i]

    second2.wait_recv()
    state = e_in[1].reshape(hh, DH, DH)
    s2[pl.ds(own, hh)] = (state + jnp.where(core == 0, loc2[1], 0.0)).astype(BF16)

    last = remote(f_out, f_in, 8, {"ctx": partner})

    @pl.when(give)
    def _():
        f_out[...] = state + jnp.where(core == 1, loc2[0], 0.0)
        last.start()

    @pl.when(take)
    def _():
        last.wait_recv()
        s2[pl.ds(other, hh)] = f_in[...].astype(BF16)

    @pl.when(jnp.logical_not(take))
    def _():
        remote(e_far, e_far, 9, {"ctx": partner}).wait_recv()
        s2[pl.ds(other, hh)] = e_far[...].reshape(hh, DH, DH).astype(BF16)

    @pl.when(give)
    def _():
        last.wait_send()

    @pl.when(core == 0)
    def _():
        n = pl.ds(0, len(quick_chips))
        remote(p_out.at[1, n], e_far.at[n], 9, {"ctx": partner}).wait_send()

    for sent in (pair, first1, swap, second1, y_all, first2, back, second2):
        sent.wait_send()


def finish(oq, og, v, lk, glk, gv, sk, s2, dq, dk, dv, dg, ok, ov, sem):
    heads = oq.shape[0]

    def put(i, src, dst, h):
        copy = pltpu.make_async_copy(src.at[h], dst.at[:, pl.ds(h * DH, DH)], sem.at[i, h])
        copy.start()
        return copy

    copies = [put(0, oq, dq, h) for h in range(heads)] + [put(1, og, dg, h) for h in range(heads)]
    for h in range(heads):
        ok[h] = ((glk[h] + mm(v[h], s2[h], NT)) * sk[h]).astype(BF16)
        copies.append(put(2, ok, dk, h))
        ov[h] = (gv[h] + mm(lk[h], s2[h], NN)).astype(BF16)
        copies.append(put(3, ov, dv, h))
    for copy in copies:
        copy.wait()


def per_device(nx, nz, nh, *args):
    rows, width = args[0].shape
    heads = width // DH
    hh = heads // 2
    chips = nx * nz
    piece = hh * DH // chips

    def vmem(dtype, *shape):
        return pltpu.VMEM(shape, dtype)

    low = vmem(BF16, heads, rows, DH)
    wide = vmem(F32, heads, rows, DH)
    low2 = vmem(BF16, hh, rows, DH)
    four = vmem(F32, 4, hh, rows, DH)
    half = vmem(F32, hh, DH, DH)
    pieces = vmem(F32, 2, chips, piece, DH)
    def shape(dtype, *dims):
        return jax.ShapeDtypeStruct(dims, dtype)

    out, out_wide = shape(BF16, heads, rows, DH), shape(F32, heads, rows, DH)
    outs = pl.pallas_call(
        functools.partial(kernel, nx, nz, nh),
        out_shape=(out, out, out, out, out_wide, out_wide, out_wide, shape(BF16, heads, DH, DH)),
        in_specs=[pl.BlockSpec(memory_space=pltpu.HBM)] * 5,
        out_specs=[pl.BlockSpec(memory_space=pltpu.VMEM)] * 8,
        scratch_shapes=[
            low, low, low, low,
            low, wide, wide,
            four, four, low2, low2, low2,
            vmem(F32, 2, hh, rows, DH), vmem(BF16, 2, hh, rows, rows), vmem(BF16, 2, hh, rows, DH),
            vmem(BF16, 2, hh, DH, DH), vmem(BF16, 2, hh, DH, rows),
            vmem(F32, heads, DH, DH), half, vmem(F32, 2, hh, DH, DH), half, half,
            pieces, pieces, pieces, pieces, vmem(F32, chips, piece, DH),
            four, four,
            vmem(F32, 2, 1, 2 * rows), vmem(F32, 2 * nh, 2, 1, 2 * rows),
            pltpu.SemaphoreType.DMA((5, heads)), pltpu.SemaphoreType.DMA((10,)), pltpu.SemaphoreType.DMA((10,)),
        ],
        compiler_params=pltpu.CompilerParams(collective_id=0, has_side_effects=True, vmem_limit_bytes=32 << 20),
        name="linear_attention",
    )(*(pltpu.with_memory_space_constraint(a, pltpu.HBM) for a in args))
    return pl.pallas_call(
        finish,
        out_shape=(shape(BF16, rows, width),) * 4,
        in_specs=[pl.BlockSpec(memory_space=pltpu.VMEM)] * 8,
        out_specs=[pl.BlockSpec(memory_space=pltpu.HBM)] * 4,
        scratch_shapes=[low, low, pltpu.SemaphoreType.DMA((4, heads))],
        compiler_params=pltpu.CompilerParams(vmem_limit_bytes=8 << 20),
        name="finish",
    )(*outs)


def solution(mesh):
    nh = mesh.shape["head"]
    nz = NZ
    nx = mesh.shape["ctx"] // (2 * nz)
    spec = P("ctx", "head")
    return jax.shard_map(
        functools.partial(per_device, nx, nz, nh),
        mesh=mesh, in_specs=(spec,) * 5, out_specs=(spec,) * 4, check_vma=False,
    )
```
